256 devices in a mesh: grp: 8 (over x, core), ep: 32 (over y, z).
Axes of the slice: x: 4, y: 4, z: 8, core: 2. Of those that a mesh axis runs over, the one named last changes fastest.
Arguments:
- queries: bfloat16 [3, 1024, 128, 576], P(None, ('grp', 'ep')), may hold values from -10 to 10, as said below
- cache: bfloat16 [1024, 128, 576], P(('grp', 'ep')), may hold values from -5 to 5, as said below
- new_entries: bfloat16 [3, 1024, 576], P(None, ('grp', 'ep')), may hold values from -5 to 5
- lengths: int32 [1024], P(('grp', 'ep')), may hold values from 2 to 125, as said below
- moe_input: bfloat16 [3, 1024, 3584], P(None, ('grp', 'ep')), may hold values from -6 to 6
- expert_ids: int32 [3, 8, 128, 8], P(None, None, 'ep'), may hold values from 0 to 31, all different within a row; in each aligned block of 4 rows (0 to 3, 4 to 7, ..., all dimensions but the last counted through in order) at most 2 rows name the same one
- route_gains: float32 [3, 8, 128, 8], P(None, None, 'ep'), may hold values from 0.1 to 1
- w_gate: bfloat16 [32, 3584, 2048], P('ep', None, 'grp'), may hold values from -0.09375 to 0.09375
- w_up: bfloat16 [32, 3584, 2048], P('ep', None, 'grp'), may hold values from -0.09375 to 0.09375
- w_down: bfloat16 [32, 2048, 3584], P('ep', 'grp'), may hold values from -0.125 to 0.125
- plan: int32 [8, 32, 2, 2], P(None, 'ep'), may hold values from 0 to 7, as said below
Outputs:
- contexts: bfloat16 [3, 1024, 128, 512], P(None, ('grp', 'ep'))
- migrated_cache: bfloat16 [1024, 128, 576], P(('grp', 'ep'))
- moe_output: bfloat16 [3, 1024, 3584], P(None, ('grp', 'ep'))
The draws below stay inside these ranges and needn't reach their ends.
Inputs may be any that keep to these rules, and one draw needn't show every extreme that they name: `queries`: queries lie in this range. `cache`: cache entries lie in this range. `lengths`: some trace has exactly 125 filled rows. `expert_ids`: within the 4 tokens of one device in one step, no expert is named by more than 2 tokens. plan[g, e, k] = (slot, grp index d): device (g, e) sends the trace in that slot to device (d, e). A device's 2 slots differ; its destinations differ from each other and from g. For each k, every device of an ep index is the destination of exactly one device's entry k, and the trace lands in the slot that the destination lists in its own entry k.
All inputs are finite; a program needn't handle non-finite values.
Results may differ from the reference program's by a relative error of at most 0.019.
Values may be sent and summed in bfloat16 or wider, within the bound.
A program may use at most 128 MiB of HBM per device.

```python
import math
import jax
import jax.numpy as jnp
import numpy as np
from jax import lax

D = 3584
HEADS = 128
LAT = 512
MOE_HID = 2048
TOPK = 8
STEPS = 3
MIG = 2
TR_DEV = 4
CAP = 128
KVDIM = 576
EXPERTS = 32
HID_DEV = 256
CAP_E = 2
TRACES = 1024
MAXLEN = 125
N_GRP = 8
N_EP = 32


def draw_queries(key, part):
    array_shape = (STEPS, TRACES, HEADS, KVDIM)
    values = jnp.clip(jax.random.normal(key, array_shape, jnp.float32), -5.0, 5.0)
    return values.astype(jnp.bfloat16)


def draw_cache(key, part):
    array_shape = (TRACES, CAP, KVDIM)
    values = jnp.clip(jax.random.normal(key, array_shape, jnp.float32), -5.0, 5.0)
    return values.astype(jnp.bfloat16)


def draw_lengths(key, part):
    key_kind, key_long, key_short, key_top = jax.random.split(key, 4)
    long_trace = jax.random.randint(key_kind, (TRACES,), 0, 4) == 0
    long_length = jax.random.randint(key_long, (TRACES,), 2, MAXLEN + 1)
    short_length = jax.random.randint(key_short, (TRACES,), 2, MAXLEN // 4 + 3)
    longest = jax.random.randint(key_top, (), 0, TRACES)
    result = jnp.where(long_trace, long_length, short_length)
    result = jnp.where(jnp.arange(TRACES) == longest, MAXLEN, result)
    return result.astype(jnp.int32)


def draw_plan(key, part):
    key_offset, key_slots = jax.random.split(key)
    offset_keys = jax.random.split(key_offset, N_EP)
    offsets = jax.vmap(lambda one_key: jax.random.permutation(one_key, N_GRP - 1)[:MIG] + 1)(offset_keys)
    slot_keys = jax.random.split(key_slots, N_GRP * N_EP)
    slots_out = jax.vmap(lambda one_key: jax.random.permutation(one_key, TR_DEV)[:MIG])(slot_keys).reshape(N_GRP, N_EP, MIG)
    destination = (jnp.arange(N_GRP)[:, None, None] + offsets[None, :, :]) % N_GRP
    return jnp.stack([slots_out, destination], axis=3).astype(jnp.int32)


def steps_of(rng, shape, shards, low, largest):
    gain = 1.0
    for position, blocks in shards:
        heights = jax.random.uniform(jax.random.fold_in(jax.random.fold_in(rng, 6), position), (blocks,), jnp.float32, low / len(shards), largest / len(shards))
        gain = gain * jnp.repeat(jnp.exp(heights), shape[position] // blocks).reshape((-1,) + (1,) * (len(shape) - 1 - position))
    return gain


def assign_block(own_key, own, number, rows, count, top, bound, slope):
    sequence = jax.random.permutation(own_key, count)
    packed, common = load_shares(count, rows * top, bound, slope, True), load_shares(count, rows * top, bound, slope, False)
    places = jnp.arange(count)

    def named(tallies, rotation):
        used = int((tallies > 0).sum())
        fixed = max(1, used // 4)
        moved = fixed + (places - fixed + rotation * (used - fixed)) % max(1, count - fixed)
        return jnp.zeros((count,), jnp.int32).at[sequence[jnp.where(places < fixed, places, moved)]].set(jnp.asarray(tallies, jnp.int32))

    tallies = jnp.where(number % 4 == 0, named(packed, number // 4), named(common, number - number // 4 - 1))
    mixed = jax.random.permutation(jax.random.fold_in(own, 3), count)
    giver, taker = mixed[0:count // 2 * 2:2], mixed[1:count // 2 * 2:2]
    room = jnp.minimum(tallies[giver] - 1, bound - tallies[taker]) // 2
    room = jnp.where((giver == sequence[0]) | (taker == sequence[0]) | (tallies[taker] == 0), 0, jnp.maximum(room, 0))
    moved = jax.random.randint(jax.random.fold_in(own, 4), (count // 2,), 0, 1 << 20) % (room + 1)
    tallies = tallies.at[giver].add(-moved).at[taker].add(moved)
    labels = jnp.searchsorted(jnp.cumsum(tallies), jnp.arange(rows * top), side="right").astype(jnp.int32)
    table = labels.reshape(top, rows).T
    table = table[jax.random.permutation(jax.random.fold_in(own, 1), rows)]
    rotation = jax.random.randint(jax.random.fold_in(own, 2), (rows, 1), 0, top)
    return jnp.take_along_axis(table, (jnp.arange(top)[None, :] + rotation) % top, axis=1)


def load_shares(amount, total, limit, skew, full):
    weights = [(1 << 20) // math.isqrt(grade ** skew) + 1 for grade in range(1, amount + 1)]
    largest = limit if full else min(limit, max(-(-total // amount), total * weights[0] // sum(weights)))
    least = 1 if total - largest >= amount - 1 else 0
    counts, rest = [largest] + [least] * (amount - 1), total - largest - least * (amount - 1)
    while rest > 0:
        candidates = [i for i in range(1, amount) if counts[i] < largest] or [i for i in range(1, amount) if counts[i] < limit]
        pool, left = sum([weights[i] for i in candidates]), rest
        for i in candidates:
            addition = min(limit - counts[i], max(1, left * weights[i] // pool), rest)
            counts[i] = counts[i] + addition
            rest = rest - addition
    return np.array(counts)


def gaussian(stream_key, extent, scale, most, shards=(), kind=jnp.bfloat16):
    values = scale * jax.random.normal(stream_key, extent, jnp.float32)
    if shards:
        values = values * steps_of(stream_key, extent, shards, -0.22, 0.18)
    return jnp.clip(values, -most, most).astype(kind)


def setup_inputs(seed: int = 0) -> dict:
    arg_keys = jax.random.split(jax.random.key(seed), 12)
    queries = draw_queries(jax.random.fold_in(arg_keys[11], 71), 0)
    cache = draw_cache(jax.random.fold_in(arg_keys[11], 71), 0)
    new_entries = gaussian(arg_keys[2], (STEPS, TRACES, KVDIM), 1.0, 5.0, ((1, 256),))
    lengths = draw_lengths(jax.random.fold_in(arg_keys[11], 71), 0)
    moe_input = gaussian(arg_keys[4], (STEPS, TRACES, D), 1.0, 6.0, ((1, 256),))
    expert_ids_keys = jax.random.split(jax.random.fold_in(arg_keys[5], 1), STEPS * N_GRP * (N_EP * TR_DEV) // TR_DEV)
    expert_ids_turns = jax.random.permutation(jax.random.fold_in(arg_keys[5], 3), STEPS * N_GRP * (N_EP * TR_DEV) // TR_DEV)
    expert_ids = jax.vmap(lambda own, number: assign_block(jax.random.fold_in(arg_keys[5], 2), own, number, TR_DEV, EXPERTS, TOPK, CAP_E, 2))(expert_ids_keys, expert_ids_turns).reshape((STEPS, N_GRP, N_EP * TR_DEV, TOPK))
    route_gains = jnp.clip(jnp.exp(math.log(1.0) - 2.3025851 * jax.random.uniform(arg_keys[6], (STEPS, N_GRP, N_EP * TR_DEV, TOPK), jnp.float32) ** steps_of(arg_keys[6], (STEPS, N_GRP, N_EP * TR_DEV, TOPK), ((2, 32),), -0.2, 0.2)), 0.1, 1.0)
    w_gate = gaussian(arg_keys[7], (EXPERTS, D, MOE_HID), D ** -0.5, 0.09375, ((0, 32), (2, 8)))
    w_up = gaussian(arg_keys[8], (EXPERTS, D, MOE_HID), D ** -0.5, 0.09375, ((0, 32), (2, 8)))
    w_down = gaussian(arg_keys[9], (EXPERTS, MOE_HID, D), MOE_HID ** -0.5, 0.125, ((0, 32), (1, 8)))
    plan = draw_plan(jax.random.fold_in(arg_keys[11], 71), 0)
    return dict(queries=queries, cache=cache, new_entries=new_entries, lengths=lengths, moe_input=moe_input, expert_ids=expert_ids, route_gains=route_gains, w_gate=w_gate, w_up=w_up, w_down=w_down, plan=plan)


SCORE_SCALE = 192.0 ** -0.5


def attend_trace(trace_index, queries, cache, new_entries, lengths):
    trace_cache = cache[trace_index]
    trace_length = lengths[trace_index]
    positions = jnp.arange(trace_cache.shape[0], dtype=jnp.int32)
    outputs = []
    for step_index in range(queries.shape[0]):
        filled = trace_length + step_index
        trace_cache = jnp.where((positions == filled)[:, None], new_entries[step_index, trace_index][None, :], trace_cache)
        scores = jnp.einsum("hd,cd->hc", queries[step_index, trace_index].astype(jnp.float32), trace_cache.astype(jnp.float32)) * SCORE_SCALE
        scores = jnp.where((positions <= filled)[None, :], scores, -jnp.inf)
        top_score = jnp.max(scores, axis=1, keepdims=True)
        exp_scores = jnp.exp(scores - top_score)
        weights = (exp_scores / jnp.sum(exp_scores, axis=1, keepdims=True)).astype(jnp.bfloat16)
        context = jnp.dot(weights, trace_cache[:, :LAT], preferred_element_type=jnp.float32)
        outputs.append(context.astype(jnp.bfloat16))
    return jnp.stack(outputs), trace_cache


def expert_layer(tokens, route_ids, route_gains, w_gate, w_up, w_down):
    most_rows = N_GRP * N_EP * CAP_E

    def per_expert(running, inputs):
        expert_index, gate_weight, up_weight, down_weight = inputs
        matched = route_ids == expert_index
        row_weight = jnp.sum(jnp.where(matched, route_gains, 0.0), axis=1)
        chosen = jnp.any(matched, axis=1)
        row_order = jnp.argsort(jnp.where(chosen, 0, 1).astype(jnp.int32), stable=True)[:most_rows].astype(jnp.int32)
        token_rows = tokens[row_order]
        gate_out = jnp.dot(token_rows, gate_weight, preferred_element_type=jnp.float32)
        up_out = jnp.dot(token_rows, up_weight, preferred_element_type=jnp.float32)
        hidden = (jax.nn.silu(gate_out) * up_out).astype(jnp.bfloat16)
        blocks = hidden.reshape(most_rows, N_GRP, HID_DEV).astype(jnp.float32)
        down_blocks = down_weight.reshape(N_GRP, HID_DEV, D).astype(jnp.float32)
        partial_sums = jnp.einsum("rbh,bhd->rbd", blocks, down_blocks, precision=lax.Precision.HIGHEST)
        partial_sums = lax.optimization_barrier(partial_sums.astype(jnp.bfloat16)).astype(jnp.float32)
        expert_out = jnp.sum(partial_sums, axis=1)
        running = running.at[row_order].add(row_weight[row_order][:, None] * expert_out)
        return running, None

    start_sum = jnp.zeros((tokens.shape[0], D), jnp.float32)
    expert_list = jnp.arange(EXPERTS, dtype=jnp.int32)
    running, unused = lax.scan(per_expert, start_sum, (expert_list, w_gate, w_up, w_down))
    return running.astype(jnp.bfloat16)


def reference(queries, cache, new_entries, lengths, moe_input, expert_ids, route_gains, w_gate, w_up, w_down, plan):
    trace_list = jnp.arange(TRACES, dtype=jnp.int32)
    contexts, grown_cache = lax.map(lambda trace_index: attend_trace(trace_index, queries, cache, new_entries, lengths), trace_list)
    contexts = jnp.transpose(contexts, (1, 0, 2, 3))
    grid_group = jnp.arange(N_GRP, dtype=jnp.int32)[:, None, None]
    grid_expert = jnp.arange(N_EP, dtype=jnp.int32)[None, :, None]
    grid_entry = jnp.arange(MIG, dtype=jnp.int32)[None, None, :]
    dest_group = plan[:, :, :, 1]
    source_index = (grid_group * N_EP + grid_expert) * TR_DEV + plan[:, :, :, 0]
    dest_slot = plan[dest_group, grid_expert, grid_entry, 0]
    dest_index = (dest_group * N_EP + grid_expert) * TR_DEV + dest_slot
    migrated_cache = grown_cache.at[dest_index.reshape(-1).astype(jnp.int32)].set(grown_cache[source_index.reshape(-1).astype(jnp.int32)])
    moe_steps = []
    for step_index in range(STEPS):
        step_ids = expert_ids[step_index].reshape(TRACES, TOPK)
        step_gains = route_gains[step_index].reshape(TRACES, TOPK)
        moe_steps.append(expert_layer(moe_input[step_index], step_ids, step_gains, w_gate, w_up, w_down))
    moe_output = jnp.stack(moe_steps)
    return contexts, migrated_cache, moe_output
```

```python
from functools import partial

import jax
import jax.numpy as jnp
from jax import lax
from jax.sharding import PartitionSpec as P

ROPE = 64


SCORE_SCALE = 192.0 ** (-0.5)


def slot_tables(route_ids, route_gains, expert_count, slot_count):
    token_count, top_count = route_ids.shape
    flat_ids = route_ids.reshape(-1)
    row_list = jnp.arange(flat_ids.shape[0], dtype=jnp.int32)
    same_expert = flat_ids[:, None] == flat_ids[None, :]
    earlier = row_list[None, :] < row_list[:, None]
    slot_rank = jnp.sum(jnp.where(same_expert & earlier, 1, 0), axis=1).astype(jnp.int32)
    slot_index = flat_ids * slot_count + slot_rank
    slot_hot = (
        slot_index[:, None] == jnp.arange(expert_count * slot_count, dtype=jnp.int32)[None, :]
    ).astype(jnp.float32)
    token_hot = (
        (row_list // top_count)[:, None] == jnp.arange(token_count, dtype=jnp.int32)[None, :]
    ).astype(jnp.float32)
    dispatch = jnp.dot(slot_hot.T, token_hot, precision=lax.Precision.HIGHEST)
    combine = jnp.dot(
        token_hot.T, slot_hot * route_gains.reshape(-1)[:, None], precision=lax.Precision.HIGHEST
    )
    return (dispatch, combine)


def expert_rows(token_rows, gate_slice, up_slice, down_slice):
    gate_out = jnp.dot(token_rows, gate_slice, preferred_element_type=jnp.float32)
    up_out = jnp.dot(token_rows, up_slice, preferred_element_type=jnp.float32)
    hidden = (jax.nn.silu(gate_out) * up_out).astype(jnp.bfloat16)
    return jnp.dot(hidden, down_slice, preferred_element_type=jnp.float32).astype(jnp.bfloat16)


def body(
    queries,
    cache,
    new_entries,
    lengths,
    moe_input,
    expert_ids,
    route_gains,
    w_gate,
    w_up,
    w_down,
    plan,
):
    trace_count = cache.shape[0]
    latent = queries.shape[3] - ROPE
    positions = jnp.arange(cache.shape[1], dtype=jnp.int32)
    grown_cache = cache
    context_list = []
    for step_index in range(queries.shape[0]):
        filled = lengths + step_index
        write_here = positions[None, :] == filled[:, None]
        grown_cache = jnp.where(
            write_here[:, :, None], new_entries[step_index][:, None, :], grown_cache
        )
        scores = (
            jnp.einsum(
                "thd,tcd->thc", queries[step_index], grown_cache, preferred_element_type=jnp.float32
            )
            * SCORE_SCALE
        )
        visible = (positions[None, :] <= filled[:, None])[:, None, :]
        scores = jnp.where(visible, scores, -jnp.inf)
        top_score = jnp.max(scores, axis=2, keepdims=True)
        exp_scores = jnp.exp(scores - top_score)
        weights = (exp_scores / jnp.sum(exp_scores, axis=2, keepdims=True)).astype(jnp.bfloat16)
        context = jnp.einsum(
            "thc,tcd->thd", weights, grown_cache[:, :, :latent], preferred_element_type=jnp.float32
        )
        context_list.append(context.astype(jnp.bfloat16))
    contexts = jnp.stack(context_list)
    groups = lax.axis_size("grp")
    group_index = lax.axis_index("grp")
    column_plan = plan[:, 0]
    own_plan = lax.dynamic_index_in_dim(column_plan, group_index, 0, keepdims=False)
    out_slots = own_plan[:, 0]
    slot_list = jnp.arange(trace_count, dtype=jnp.int32)
    leaving = (out_slots[None, :] == slot_list[:, None]).astype(jnp.float32)
    arriving = (column_plan[:, :, 1] == group_index).astype(jnp.float32)
    keep_slot = jnp.sum(leaving, axis=1) < 0.5
    outgoing = jnp.einsum(
        "tk,tcd->kcd", leaving.astype(jnp.bfloat16), grown_cache, preferred_element_type=jnp.float32
    ).astype(jnp.bfloat16)
    received = lax.all_gather(outgoing, "grp", axis=0, tiled=True)
    placement = (
        (leaving[:, None, :] * arriving[None, :, :]).reshape(trace_count, -1).astype(jnp.bfloat16)
    )
    incoming = jnp.einsum("ts,scd->tcd", placement, received, preferred_element_type=jnp.float32)
    migrated_cache = jnp.where(keep_slot[:, None, None], grown_cache, incoming.astype(jnp.bfloat16))
    experts = lax.axis_size("ep")
    step_count = moe_input.shape[0]
    model_width = moe_input.shape[2]
    slot_count = 2
    tables = partial(slot_tables, expert_count=experts, slot_count=slot_count)
    own_ids = lax.dynamic_index_in_dim(expert_ids, group_index, 1, keepdims=False)
    own_gains = lax.dynamic_index_in_dim(route_gains, group_index, 1, keepdims=False)
    dispatch_own, combine_own = jax.vmap(tables)(own_ids, own_gains)
    packed = jnp.einsum(
        "nsj,njd->snd",
        dispatch_own.astype(jnp.bfloat16),
        moe_input,
        preferred_element_type=jnp.float32,
    ).astype(jnp.bfloat16)
    packed = packed.reshape(experts, slot_count * step_count, model_width)
    exchanged = lax.all_to_all(packed, "ep", split_axis=0, concat_axis=0, tiled=True)
    own_rows = exchanged.reshape(-1, model_width)
    all_rows = lax.all_gather(own_rows, "grp", axis=0, tiled=True)
    partial_out = expert_rows(all_rows, w_gate[0], w_up[0], w_down[0])
    summed = lax.psum_scatter(partial_out, "grp", scatter_dimension=0, tiled=True)
    returned = lax.all_to_all(
        summed.reshape(exchanged.shape), "ep", split_axis=0, concat_axis=0, tiled=True
    )
    returned = returned.reshape(experts * slot_count, step_count, model_width)
    moe_output = jnp.einsum(
        "njs,snd->njd", combine_own, returned.astype(jnp.float32), precision=lax.Precision.HIGHEST
    ).astype(jnp.bfloat16)
    return (contexts, migrated_cache, moe_output)


def solution(mesh):
    return jax.shard_map(
        body,
        mesh=mesh,
        in_specs=(
            P(None, ("grp", "ep"), None, None),
            P(("grp", "ep"), None, None),
            P(None, ("grp", "ep"), None),
            P(("grp", "ep")),
            P(None, ("grp", "ep"), None),
            P(None, None, "ep", None),
            P(None, None, "ep", None),
            P("ep", None, "grp"),
            P("ep", None, "grp"),
            P("ep", "grp", None),
            P(None, "ep", None, None),
        ),
        out_specs=(
            P(None, ("grp", "ep"), None, None),
            P(("grp", "ep"), None, None),
            P(None, ("grp", "ep"), None),
        ),
        check_vma=False,
    )
```

```python
from functools import partial

import jax
import jax.numpy as jnp
from jax import lax
from jax.experimental import pallas as pl
from jax.experimental.pallas import tpu as pltpu
from jax.sharding import PartitionSpec as P

ROPE = 64
SCORE_SCALE = 192.0 ** (-0.5)
NX = 4
NY = 4
NQ = 4
CAP_E = 2
MESH = pl.DeviceIdType.MESH


def attention_kernel(lengths, queries, cache, entries, contexts, grown):
    trace = pl.program_id(0)
    steps, latent = queries.shape[0], contexts.shape[3]
    keys = cache[0]
    filled = lengths[trace]
    row = lax.broadcasted_iota(jnp.int32, (keys.shape[0], 1), 0)
    column = lax.broadcasted_iota(jnp.int32, (1, keys.shape[0]), 1)
    for step in range(steps):
        entry = entries[step, 0]
        keys = jnp.where(row == filled + step, entry, keys)
        scores = lax.dot_general(
            queries[step, 0], keys, (((1,), (1,)), ((), ())), preferred_element_type=jnp.float32
        )
        scores = jnp.where(column <= filled + step, scores * SCORE_SCALE, -jnp.inf)
        grown_exp = jnp.exp(scores - jnp.max(scores, axis=1, keepdims=True))
        weights = grown_exp / jnp.sum(grown_exp, axis=1, keepdims=True)
        contexts[step, 0] = jnp.dot(
            weights.astype(jnp.bfloat16), keys[:, :latent], preferred_element_type=jnp.float32
        ).astype(jnp.bfloat16)
    grown[0] = keys


def attention(lengths, queries, cache, entries):
    steps, traces, heads, width = queries.shape
    rows, latent = cache.shape[1], width - ROPE
    return pl.pallas_call(
        attention_kernel,
        grid_spec=pltpu.PrefetchScalarGridSpec(
            num_scalar_prefetch=1,
            grid=(traces,),
            in_specs=[
                pl.BlockSpec((steps, 1, heads, width), lambda t, n: (0, t, 0, 0)),
                pl.BlockSpec((1, rows, width), lambda t, n: (t, 0, 0)),
                pl.BlockSpec((steps, 1, 1, width), lambda t, n: (0, t, 0, 0)),
            ],
            out_specs=[
                pl.BlockSpec((steps, 1, heads, latent), lambda t, n: (0, t, 0, 0)),
                pl.BlockSpec((1, rows, width), lambda t, n: (t, 0, 0)),
            ],
        ),
        out_shape=[
            jax.ShapeDtypeStruct((steps, traces, heads, latent), jnp.bfloat16),
            jax.ShapeDtypeStruct(cache.shape, cache.dtype),
        ],
        compiler_params=pltpu.CompilerParams(vmem_limit_bytes=16 << 20),
        cost_estimate=pl.CostEstimate(
            flops=2 * steps * traces * heads * rows * (width + latent),
            bytes_accessed=8 << 20,
            transcendentals=steps * traces * heads * rows,
        ),
    )(lengths, queries, cache, entries[:, :, None, :])


def expert_kernel(
    ny, nz, tokens, rank_row, route_col, wg_hbm, wu_hbm, wd_hbm, out,
    wg, wu, wd, tb, xb, pb, r1, ra, rb, yb, db, yr, eb, zr, wsem, send_sems, recv_sems,
):
    steps = tokens.shape[0]
    block, quarter = tokens.shape[1], tokens.shape[2]
    cap = xb.shape[2]
    half = cap // 2
    group, expert = lax.axis_index("grp"), lax.axis_index("ep")
    x, c = group // 2, group % 2
    y, z = expert // nz, expert % nz
    right, left, far = (x + 1) % NX, (x + NX - 1) % NX, (x + 2) % NX
    dev_right, dev_left = (right * 2 + c, expert), (left * 2 + c, expert)
    dev_sib = (x * 2 + 1 - c, expert)

    def dev_y(k):
        return (group, ((y + k) % ny) * nz + z)

    def dev_z(k):
        return (group, y * nz + (z + k) % nz)

    peers = [dev_right, dev_left, dev_sib]
    peers += [dev_y(k) for k in range(1, ny)] + [dev_z(k) for k in range(1, nz)]
    barrier = pltpu.get_barrier_semaphore()
    for peer in peers:
        pl.semaphore_signal(barrier, inc=1, device_id=peer, device_id_type=MESH)
    loads = [
        pltpu.make_async_copy(hbm.at[0], vmem, wsem.at[i])
        for i, (hbm, vmem) in enumerate(((wg_hbm, wg), (wu_hbm, wu), (wd_hbm, wd)))
    ]
    for load in loads:
        load.start()
    pl.semaphore_wait(barrier, len(peers))

    number = {}
    started = []

    def slot(tag):
        return number.setdefault(tag, len(number))

    def send(tag, src, dst, dev):
        i = slot(tag)
        copy = pltpu.make_async_remote_copy(
            src_ref=src, dst_ref=dst, send_sem=send_sems.at[i], recv_sem=recv_sems.at[i],
            device_id=dev, device_id_type=MESH,
        )
        copy.start()
        started.append(copy)

    def arrived(tag, dst):
        i = slot(tag)
        pltpu.make_async_remote_copy(
            src_ref=dst, dst_ref=dst, send_sem=send_sems.at[i], recv_sem=recv_sems.at[i],
            device_id=dev_right, device_id_type=MESH,
        ).wait_recv()

    def z_send(s):
        tb[s, expert] = tokens[s]
        for k in range(1, nz):
            send(("z", s, k), tb.at[s, expert], tb.at[s, expert], dev_z(k))

    def z_wait(s):
        for k in range(1, nz):
            arrived(("z", s, k), tb.at[s, y * nz + (z + nz - k) % nz])

    def y_send(s):
        part = tb.at[s, pl.ds(y * nz, nz)]
        for k in range(1, ny):
            send(("y", s, k), part, part, dev_y(k))

    def y_wait(s):
        for k in range(1, ny):
            arrived(("y", s, k), tb.at[s, pl.ds(((y + ny - k) % ny) * nz, nz)])

    columns = ny * nz * block

    def select(s):
        want = lax.broadcasted_iota(jnp.int32, (NQ * cap, columns), 0)
        lane = lax.broadcasted_iota(jnp.int32, (NQ * cap, columns), 1)
        pick = (rank_row[s] == want % cap) & ((lane // (block // NQ)) % NQ == want // cap)
        pick = jnp.where(pick, 1.0, 0.0).astype(jnp.bfloat16)
        rows = jnp.dot(
            pick, tb[s].reshape(columns, quarter), preferred_element_type=jnp.float32
        ).astype(jnp.bfloat16)
        for q in range(NQ):
            xb[s, c * NX + x, :, q * quarter:(q + 1) * quarter] = rows[q * cap:(q + 1) * cap]

    low, high = pl.ds(0, half), pl.ds(half, half)

    def x_own(s):
        mine = xb.at[s, c * NX + x]
        send(("xl", s), mine, mine, dev_right)
        send(("xr", s), mine, mine, dev_left)
        send(("so", s), mine, mine, dev_sib)

    def x_near(s):
        from_left, from_right = c * NX + left, c * NX + right
        arrived(("xl", s), xb.at[s, from_left])
        send(("x2l", s), xb.at[s, from_left, low], xb.at[s, from_left, low], dev_right)
        send(("sl", s), xb.at[s, from_left], xb.at[s, from_left], dev_sib)
        arrived(("xr", s), xb.at[s, from_right])
        send(("x2r", s), xb.at[s, from_right, high], xb.at[s, from_right, high], dev_left)
        send(("sr", s), xb.at[s, from_right], xb.at[s, from_right], dev_sib)

    def x_all(s):
        across, other = c * NX + far, (1 - c) * NX
        arrived(("x2l", s), xb.at[s, across, low])
        send(("s2l", s), xb.at[s, across, low], xb.at[s, across, low], dev_sib)
        arrived(("x2r", s), xb.at[s, across, high])
        send(("s2r", s), xb.at[s, across, high], xb.at[s, across, high], dev_sib)
        arrived(("so", s), xb.at[s, other + x])
        arrived(("sl", s), xb.at[s, other + left])
        arrived(("sr", s), xb.at[s, other + right])
        arrived(("s2l", s), xb.at[s, other + far, low])
        arrived(("s2r", s), xb.at[s, other + far, high])

    def experts(s):
        def part(h, carry):
            rows = xb[s, pl.ds(h * NX, NX)].reshape(NX * cap, NQ * quarter)
            gate = jnp.dot(rows, wg[...], preferred_element_type=jnp.float32)
            up = jnp.dot(rows, wu[...], preferred_element_type=jnp.float32)
            hidden = (gate / (1.0 + jnp.exp(-gate)) * up).astype(jnp.bfloat16)
            for q in range(NQ):
                cols = slice(q * quarter, (q + 1) * quarter)
                pb[s, pl.ds(h * NX, NX), :, cols] = (
                    jnp.dot(hidden, wd[:, cols], preferred_element_type=jnp.float32)
                    .astype(jnp.bfloat16).reshape(NX, cap, quarter)
                )
            return carry

        lax.fori_loop(0, 2, part, 0)
        send(("r1", s), pb.at[s, pl.ds((1 - c) * NX, NX)], r1.at[s], dev_sib)

    piece = 16

    def add_into(dst, other, first, rows):
        def part(i, carry):
            at = pl.ds(pl.multiple_of(first + i * piece, piece), piece)
            inner = pl.ds(pl.multiple_of(i * piece, piece), piece)
            at_other = at if other.shape[0] == cap else inner
            total = dst[at].astype(jnp.float32) + other[at_other].astype(jnp.float32)
            dst[at] = total.astype(jnp.bfloat16)
            return carry

        lax.fori_loop(0, rows // piece, part, 0)

    def r1_add(s):
        arrived(("r1", s), r1.at[s])
        to_far, to_right, to_left = c * NX + far, c * NX + right, c * NX + left
        add_into(pb.at[s, to_far], r1.at[s, far], 0, cap)
        send(("ral", s), pb.at[s, to_far, low], ra.at[s, 0], dev_right)
        send(("rar", s), pb.at[s, to_far, high], ra.at[s, 1], dev_left)
        add_into(pb.at[s, to_right], r1.at[s, right], 0, cap)
        send(("rbl", s, 1), pb.at[s, to_right, high], rb.at[s, 0, high], dev_right)
        add_into(pb.at[s, to_left], r1.at[s, left], 0, cap)
        send(("rbr", s, 0), pb.at[s, to_left, low], rb.at[s, 1, low], dev_left)

    def ra_add(s):
        to_right, to_left = c * NX + right, c * NX + left
        arrived(("ral", s), ra.at[s, 0])
        add_into(pb.at[s, to_right], ra.at[s, 0], 0, half)
        send(("rbl", s, 0), pb.at[s, to_right, low], rb.at[s, 0, low], dev_right)
        arrived(("rar", s), ra.at[s, 1])
        add_into(pb.at[s, to_left], ra.at[s, 1], half, half)
        send(("rbr", s, 1), pb.at[s, to_left, high], rb.at[s, 1, high], dev_left)

    def combine(s):
        arrived(("rbl", s, 1), rb.at[s, 0, high])
        arrived(("rbr", s, 0), rb.at[s, 1, low])
        arrived(("rbl", s, 0), rb.at[s, 0, low])
        arrived(("rbr", s, 1), rb.at[s, 1, high])

        def final(i, carry):
            at = pl.ds(pl.multiple_of(i * piece, piece), piece)
            total = pb[s, c * NX + x, at].astype(jnp.float32) + r1[s, x, at].astype(jnp.float32)
            total += rb[s, 0, at].astype(jnp.float32) + rb[s, 1, at].astype(jnp.float32)
            total = total.astype(jnp.bfloat16)
            for q in range(NQ):
                to = pl.ds(pl.multiple_of(q * cap + i * piece, piece), piece)
                yb[to, :] = total[:, q * quarter:(q + 1) * quarter]
            return carry

        lax.fori_loop(0, cap // piece, final, 0)
        rows = nz * block

        def part(i, carry):
            route = route_col[s, pl.ds(pl.multiple_of(i * rows, rows), rows), :]
            sub = lax.broadcasted_iota(jnp.int32, (rows, NQ * cap), 0)
            lane = lax.broadcasted_iota(jnp.int32, (rows, NQ * cap), 1)
            mine = (route[:, 0:1] == (lane % cap).astype(jnp.float32)) & (
                (sub // (block // NQ)) % NQ == lane // cap
            )
            gain = jnp.where(mine, route[:, 1:2], 0.0)
            coarse = gain.astype(jnp.bfloat16)
            fine = (gain - coarse.astype(jnp.float32)).astype(jnp.bfloat16)
            total = jnp.dot(coarse, yb[...], preferred_element_type=jnp.float32)
            total += jnp.dot(fine, yb[...], preferred_element_type=jnp.float32)
            db[s, pl.ds(i * nz, nz)] = total.astype(jnp.bfloat16).reshape(nz, block, quarter)
            return carry

        lax.fori_loop(0, ny, part, 0)
        for k in range(1, ny):
            send(("yr", s, k), db.at[s, pl.ds(((y + k) % ny) * nz, nz)], yr.at[s, k - 1], dev_y(k))

    def y_sum(s):
        for k in range(1, ny):
            arrived(("yr", s, k), yr.at[s, k - 1])

        def part(i, carry):
            total = db[s, y * nz + i].astype(jnp.float32)
            for k in range(1, ny):
                total += yr[s, k - 1, i].astype(jnp.float32)
            eb[s, i] = total.astype(jnp.bfloat16)
            return carry

        lax.fori_loop(0, nz, part, 0)
        for k in range(1, nz):
            send(("zr", s, k), eb.at[s, (z + k) % nz], zr.at[s, k - 1], dev_z(k))

    def z_sum(s):
        total = eb[s, z].astype(jnp.float32)
        for k in range(1, nz):
            arrived(("zr", s, k), zr.at[s, k - 1])
            total += zr[s, k - 1].astype(jnp.float32)
        out[s] = total.astype(jnp.bfloat16)

    for s in range(steps):
        z_send(s)
    for s in range(steps):
        z_wait(s)
        y_send(s)
    y_wait(0), select(0), x_own(0)
    x_near(0)
    y_wait(1), select(1), x_own(1)
    x_all(0)
    for load in loads:
        load.wait()
    experts(0)
    x_near(1)
    y_wait(2), select(2), x_own(2)
    r1_add(0)
    x_all(1)
    experts(1)
    ra_add(0)
    x_near(2)
    r1_add(1)
    x_all(2)
    experts(2)
    combine(0)
    ra_add(1)
    r1_add(2)
    y_sum(0)
    combine(1)
    ra_add(2)
    z_sum(0)
    y_sum(1)
    combine(2)
    z_sum(1)
    y_sum(2)
    z_sum(2)
    for copy in started:
        copy.wait_send()


def expert_copies(steps, ny, nz):
    return steps * (2 * (ny - 1) + 2 * (nz - 1) + 9 + 7)


def expert_call(tokens, rank_row, route_col, w_gate, w_up, w_down, ny, nz):
    steps, block, quarter = tokens.shape
    cap = ny * nz * CAP_E
    width, hidden = w_gate.shape[1], w_gate.shape[2]
    copies = expert_copies(steps, ny, nz)
    bf16 = jnp.bfloat16
    any_spec = pl.BlockSpec(memory_space=pl.ANY)
    vmem_spec = pl.BlockSpec(memory_space=pltpu.VMEM)
    return pl.pallas_call(
        partial(expert_kernel, ny, nz),
        in_specs=[vmem_spec] * 3 + [any_spec] * 3,
        out_specs=vmem_spec,
        out_shape=jax.ShapeDtypeStruct(tokens.shape, bf16),
        scratch_shapes=[
            pltpu.VMEM((width, hidden), bf16),
            pltpu.VMEM((width, hidden), bf16),
            pltpu.VMEM((hidden, width), bf16),
            pltpu.VMEM((steps, ny * nz, block, quarter), bf16),
            pltpu.VMEM((steps, 2 * NX, cap, width), bf16),
            pltpu.VMEM((steps, 2 * NX, cap, width), bf16),
            pltpu.VMEM((steps, NX, cap, width), bf16),
            pltpu.VMEM((steps, 2, cap // 2, width), bf16),
            pltpu.VMEM((steps, 2, cap, width), bf16),
            pltpu.VMEM((NQ * cap, quarter), bf16),
            pltpu.VMEM((steps, ny * nz, block, quarter), bf16),
            pltpu.VMEM((steps, max(ny - 1, 1), nz, block, quarter), bf16),
            pltpu.VMEM((steps, nz, block, quarter), bf16),
            pltpu.VMEM((steps, max(nz - 1, 1), block, quarter), bf16),
            pltpu.SemaphoreType.DMA((3,)),
            pltpu.SemaphoreType.DMA((copies,)),
            pltpu.SemaphoreType.DMA((copies,)),
        ],
        compiler_params=pltpu.CompilerParams(
            collective_id=0, has_side_effects=True, vmem_limit_bytes=60 << 20
        ),
    )(tokens, rank_row, route_col, w_gate, w_up, w_down)


def moe(moe_input, expert_ids, route_gains, w_gate, w_up, w_down, ny):
    group, expert = lax.axis_index("grp"), lax.axis_index("ep")
    nz = lax.axis_size("ep") // ny
    steps, owned, width = moe_input.shape
    quarter = width // NQ
    own_ids = lax.dynamic_index_in_dim(expert_ids, group, 1, keepdims=False)
    own_gains = lax.dynamic_index_in_dim(route_gains, group, 1, keepdims=False)
    routes = jnp.stack([own_ids.astype(jnp.float32), own_gains]).reshape(1, -1)
    routes = lax.all_gather(routes, "ep", axis=0, tiled=True)
    routes = routes.reshape((ny * nz, 2) + own_ids.shape)
    hit = routes[:, 0] == expert.astype(jnp.float32)
    gain = jnp.sum(jnp.where(hit, routes[:, 1], 0.0), axis=3)
    chosen = jnp.any(hit, axis=3)
    chosen = jnp.swapaxes(chosen, 0, 1).reshape(steps, -1)
    gain = jnp.swapaxes(gain, 0, 1)
    index = jnp.arange(chosen.shape[1], dtype=jnp.int32)
    before = (chosen[:, None, :] & (index[None, :] < index[:, None])[None]).astype(jnp.int32)
    rank = jnp.where(chosen, jnp.sum(before, axis=2), -1).reshape(steps, ny * nz, owned)

    def spread(value):
        value = jnp.broadcast_to(value[:, :, None, :], (steps, ny * nz, NQ, owned))
        return value.reshape(steps, -1)

    rank_row = spread(rank)[:, None, :]
    route_col = jnp.stack([spread(rank.astype(jnp.float32)), spread(gain)], axis=2)
    tokens = jnp.swapaxes(moe_input.reshape(steps, owned, NQ, quarter), 1, 2)
    tokens = tokens.reshape(steps, NQ * owned, quarter)
    out = expert_call(tokens, rank_row, route_col, w_gate, w_up, w_down, ny, nz)
    out = jnp.swapaxes(out.reshape(steps, NQ, owned, quarter), 1, 2)
    return out.reshape(steps, owned, width)


def migrate(grown, plan):
    group = lax.axis_index("grp")
    column = plan[:, 0]
    entries = column.shape[1]
    own = lax.dynamic_index_in_dim(column, group, 0, keepdims=False)
    outgoing = jnp.stack(
        [lax.dynamic_index_in_dim(grown, own[k, 0], 0, keepdims=False) for k in range(entries)]
    )
    received = lax.all_gather(outgoing, "grp", axis=0, tiled=True)
    result = grown
    for k in range(entries):
        source = jnp.sum(
            jnp.where(column[:, k, 1] == group, jnp.arange(column.shape[0], dtype=jnp.int32), 0)
        )
        incoming = lax.dynamic_index_in_dim(received, source * entries + k, 0, keepdims=True)
        result = lax.dynamic_update_slice(result, incoming, (own[k, 0], 0, 0))
    return result


def body(
    ny, queries, cache, new_entries, lengths, moe_input, expert_ids, route_gains,
    w_gate, w_up, w_down, plan,
):
    contexts, grown = attention(lengths, queries, cache, new_entries)
    moe_output = moe(moe_input, expert_ids, route_gains, w_gate, w_up, w_down, ny)
    migrated_cache = migrate(grown, plan)
    return (contexts, migrated_cache, moe_output)


def solution(mesh):
    return jax.shard_map(
        partial(body, NY),
        mesh=mesh,
        in_specs=(
            P(None, ("grp", "ep"), None, None),
            P(("grp", "ep"), None, None),
            P(None, ("grp", "ep"), None),
            P(("grp", "ep")),
            P(None, ("grp", "ep"), None),
            P(None, None, "ep", None),
            P(None, None, "ep", None),
            P("ep", None, "grp"),
            P("ep", None, "grp"),
            P("ep", "grp", None),
            P(None, "ep", None, None),
        ),
        out_specs=(
            P(None, ("grp", "ep"), None, None),
            P(("grp", "ep"), None, None),
            P(None, ("grp", "ep"), None),
        ),
        check_vma=False,
    )
```

```python
from functools import partial

import jax
import jax.numpy as jnp
from jax import lax
from jax.experimental import pallas as pl
from jax.experimental.pallas import tpu as pltpu
from jax.sharding import PartitionSpec as P

ROPE = 64
SCORE_SCALE = 192.0 ** (-0.5)
NX = 4
NY = 4
NQ = 4
CAP_E = 2
MESH = pl.DeviceIdType.MESH


def attention_kernel(lengths, queries, cache, entries, contexts, grown):
    filled = lengths[pl.program_id(0)]
    steps, latent = queries.shape[0], contexts.shape[3]
    rows = cache.shape[2]
    at_row = lax.broadcasted_iota(jnp.int32, (entries.shape[1], rows), 1) - filled
    step_of = lax.broadcasted_iota(jnp.int32, (entries.shape[1], rows), 0)
    place = jnp.where((at_row == step_of) & (step_of < steps), 1.0, 0.0).astype(jnp.bfloat16)
    added = lax.dot_general(
        entries[0], place, (((0,), (0,)), ((), ())), preferred_element_type=jnp.float32
    )
    lane = lax.broadcasted_iota(jnp.int32, (1, rows), 1) - filled
    old = cache[0].astype(jnp.float32)
    keys = jnp.where((lane >= 0) & (lane < steps), added, old)
    grown[0] = keys.astype(jnp.bfloat16)
    keys = keys.T.astype(jnp.bfloat16)
    position = lax.broadcasted_iota(jnp.int32, (rows, 1), 0) - filled
    for step in range(steps):
        scores = jnp.dot(keys, queries[step, 0], preferred_element_type=jnp.float32)
        scores = jnp.where(position <= step, scores * SCORE_SCALE, -jnp.inf)
        raised = jnp.exp(scores - jnp.max(scores, axis=0, keepdims=True))
        weights = raised / jnp.sum(raised, axis=0, keepdims=True)
        contexts[step, 0] = jnp.dot(
            weights.T.astype(jnp.bfloat16), keys[:, :latent], preferred_element_type=jnp.float32
        ).astype(jnp.bfloat16)


def attention(lengths, queries, cache, entries):
    steps, traces, width, heads = queries.shape
    rows, latent = cache.shape[2], width - ROPE
    entries = jnp.pad(jnp.swapaxes(entries, 0, 1), ((0, 0), (0, 16 - steps), (0, 0)))
    return pl.pallas_call(
        attention_kernel,
        grid_spec=pltpu.PrefetchScalarGridSpec(
            num_scalar_prefetch=1,
            grid=(traces,),
            in_specs=[
                pl.BlockSpec((steps, 1, width, heads), lambda t, n: (0, t, 0, 0)),
                pl.BlockSpec((1, width, rows), lambda t, n: (t, 0, 0)),
                pl.BlockSpec((1, 16, width), lambda t, n: (t, 0, 0)),
            ],
            out_specs=[
                pl.BlockSpec((steps, 1, heads, latent), lambda t, n: (0, t, 0, 0)),
                pl.BlockSpec((1, width, rows), lambda t, n: (t, 0, 0)),
            ],
        ),
        out_shape=[
            jax.ShapeDtypeStruct((steps, traces, heads, latent), jnp.bfloat16),
            jax.ShapeDtypeStruct(cache.shape, cache.dtype),
        ],
        compiler_params=pltpu.CompilerParams(vmem_limit_bytes=16 << 20),
        cost_estimate=pl.CostEstimate(
            flops=2 * steps * traces * heads * rows * (width + latent),
            bytes_accessed=8 << 20,
            transcendentals=steps * traces * heads * rows,
        ),
    )(lengths, queries, cache, entries)


def expert_kernel(
    ny, nz, top, tokens, routes, wg_hbm, wu_hbm, wd_hbm, out,
    wg, wu, wd, rt, tri, rank_col, gain_col, tb, xb, pb, r1, ra, rb, yb, db, yr, eb, zr, wsem, send_sems, recv_sems,
):
    steps = tokens.shape[0]
    block, quarter = tokens.shape[1], tokens.shape[2]
    cap = xb.shape[2]
    half = cap // 2
    group, expert = lax.axis_index("grp"), lax.axis_index("ep")
    x, c = group // 2, group % 2
    y, z = expert // nz, expert % nz
    right, left, far = (x + 1) % NX, (x + NX - 1) % NX, (x + 2) % NX
    dev_right, dev_left = (right * 2 + c, expert), (left * 2 + c, expert)
    dev_sib = (x * 2 + 1 - c, expert)

    def dev_y(k):
        return (group, ((y + k) % ny) * nz + z)

    def dev_z(k):
        return (group, y * nz + (z + k) % nz)

    peers = [dev_right, dev_left, dev_sib]
    peers += [dev_y(k) for k in range(1, ny)] + [dev_z(k) for k in range(1, nz)]
    barrier = pltpu.get_barrier_semaphore()
    for peer in peers:
        pl.semaphore_signal(barrier, inc=1, device_id=peer, device_id_type=MESH)
    loads = [
        pltpu.make_async_copy(hbm.at[0], vmem, wsem.at[i])
        for i, (hbm, vmem) in enumerate(((wg_hbm, wg), (wu_hbm, wu), (wd_hbm, wd)))
    ]
    for load in loads:
        load.start()
    pl.semaphore_wait(barrier, len(peers))

    number = {}
    started = []

    def slot(tag):
        return number.setdefault(tag, len(number))

    def send(tag, src, dst, dev):
        i = slot(tag)
        copy = pltpu.make_async_remote_copy(
            src_ref=src, dst_ref=dst, send_sem=send_sems.at[i], recv_sem=recv_sems.at[i],
            device_id=dev, device_id_type=MESH,
        )
        copy.start()
        started.append(copy)

    def arrived(tag, dst):
        i = slot(tag)
        pltpu.make_async_remote_copy(
            src_ref=dst, dst_ref=dst, send_sem=send_sems.at[i], recv_sem=recv_sems.at[i],
            device_id=dev_right, device_id_type=MESH,
        ).wait_recv()

    def route_z_send():
        rt[expert] = routes[...]
        for k in range(1, nz):
            send(("rz", k), rt.at[expert], rt.at[expert], dev_z(k))

    def route_y_send():
        for k in range(1, nz):
            arrived(("rz", k), rt.at[y * nz + (z + nz - k) % nz])
        part = rt.at[pl.ds(y * nz, nz)]
        for k in range(1, ny):
            send(("ry", k), part, part, dev_y(k))

    def z_send(s):
        tb[s, expert] = tokens[s]
        for k in range(1, nz):
            send(("z", s, k), tb.at[s, expert], tb.at[s, expert], dev_z(k))

    def z_wait(s):
        for k in range(1, nz):
            arrived(("z", s, k), tb.at[s, y * nz + (z + nz - k) % nz])

    def y_send(s):
        part = tb.at[s, pl.ds(y * nz, nz)]
        for k in range(1, ny):
            send(("y", s, k), part, part, dev_y(k))

    def y_wait(s):
        for k in range(1, ny):
            arrived(("y", s, k), tb.at[s, pl.ds(((y + ny - k) % ny) * nz, nz)])

    columns = ny * nz * block
    owned = block // NQ

    def earlier():
        row = lax.broadcasted_iota(jnp.int32, (columns, columns), 0)
        other = lax.broadcasted_iota(jnp.int32, (columns, columns), 1)
        row_token = row // block * owned + row % owned
        other_token = other // block * owned + other % owned
        counted = ((other // owned) % NQ == 0) & (other_token < row_token)
        tri[...] = jnp.where(counted, 1.0, 0.0).astype(jnp.bfloat16)

    def rank(s):
        if s == 0:
            for k in range(1, ny):
                arrived(("ry", k), rt.at[pl.ds(((y + ny - k) % ny) * nz, nz)])
        route = rt[:, s].reshape(columns, rt.shape[3])
        lane = lax.broadcasted_iota(jnp.int32, route.shape, 1)
        hit = (route == expert.astype(jnp.float32)) & (lane < top)
        gains = pltpu.roll(route, rt.shape[3] - top, 1)
        gain = jnp.sum(jnp.where(hit, gains, 0.0), axis=1, keepdims=True)
        chosen = jnp.sum(jnp.where(hit, 1.0, 0.0), axis=1, keepdims=True)
        chosen = jnp.broadcast_to(chosen, route.shape)
        before = jnp.dot(tri[...], chosen.astype(jnp.bfloat16), preferred_element_type=jnp.float32)
        rank_col[s] = jnp.where(chosen > 0.5, before, -1.0)
        gain_col[s] = jnp.broadcast_to(gain, route.shape)

    def slots_of(s, first, rows):
        at = pl.ds(first, rows)
        sub = lax.broadcasted_iota(jnp.int32, (rows, NQ * cap), 0)
        lane = lax.broadcasted_iota(jnp.int32, (rows, NQ * cap), 1)
        return (rank_col[s, at, 0:1] == (lane % cap).astype(jnp.float32)) & (
            (sub // owned) % NQ == lane // cap
        )

    def select(s):
        rank(s)
        pick = jnp.where(slots_of(s, 0, columns), 1.0, 0.0).astype(jnp.bfloat16)
        rows = lax.dot_general(
            pick, tb[s].reshape(columns, quarter), (((0,), (0,)), ((), ())),
            preferred_element_type=jnp.float32,
        ).astype(jnp.bfloat16)
        for q in range(NQ):
            xb[s, c * NX + x, :, q * quarter:(q + 1) * quarter] = rows[q * cap:(q + 1) * cap]

    low, high = pl.ds(0, half), pl.ds(half, half)

    def x_own(s):
        mine = xb.at[s, c * NX + x]
        send(("xl", s), mine, mine, dev_right)
        send(("xr", s), mine, mine, dev_left)
        send(("so", s), mine, mine, dev_sib)

    def x_near(s):
        from_left, from_right = c * NX + left, c * NX + right
        arrived(("xl", s), xb.at[s, from_left])
        send(("x2l", s), xb.at[s, from_left, low], xb.at[s, from_left, low], dev_right)
        send(("sl", s), xb.at[s, from_left], xb.at[s, from_left], dev_sib)
        arrived(("xr", s), xb.at[s, from_right])
        send(("x2r", s), xb.at[s, from_right, high], xb.at[s, from_right, high], dev_left)
        send(("sr", s), xb.at[s, from_right], xb.at[s, from_right], dev_sib)

    def x_all(s):
        across, other = c * NX + far, (1 - c) * NX
        arrived(("x2l", s), xb.at[s, across, low])
        send(("s2l", s), xb.at[s, across, low], xb.at[s, across, low], dev_sib)
        arrived(("x2r", s), xb.at[s, across, high])
        send(("s2r", s), xb.at[s, across, high], xb.at[s, across, high], dev_sib)
        arrived(("so", s), xb.at[s, other + x])
        arrived(("sl", s), xb.at[s, other + left])
        arrived(("sr", s), xb.at[s, other + right])
        arrived(("s2l", s), xb.at[s, other + far, low])
        arrived(("s2r", s), xb.at[s, other + far, high])

    def experts(s):
        def part(h, carry):
            rows = xb[s, pl.ds(h * NX, NX)].reshape(NX * cap, NQ * quarter)
            gate = jnp.dot(rows, wg[...], preferred_element_type=jnp.float32)
            up = jnp.dot(rows, wu[...], preferred_element_type=jnp.float32)
            hidden = (gate / (1.0 + jnp.exp(-gate)) * up).astype(jnp.bfloat16)
            for q in range(NQ):
                cols = slice(q * quarter, (q + 1) * quarter)
                pb[s, pl.ds(h * NX, NX), :, cols] = (
                    jnp.dot(hidden, wd[:, cols], preferred_element_type=jnp.float32)
                    .astype(jnp.bfloat16).reshape(NX, cap, quarter)
                )
            return carry

        lax.fori_loop(0, 2, part, 0)
        send(("r1", s), pb.at[s, pl.ds((1 - c) * NX, NX)], r1.at[s], dev_sib)

    piece = 16

    def add_into(dst, other, first, rows):
        def part(i, carry):
            at = pl.ds(pl.multiple_of(first + i * piece, piece), piece)
            inner = pl.ds(pl.multiple_of(i * piece, piece), piece)
            at_other = at if other.shape[0] == cap else inner
            total = dst[at].astype(jnp.float32) + other[at_other].astype(jnp.float32)
            dst[at] = total.astype(jnp.bfloat16)
            return carry

        lax.fori_loop(0, rows // piece, part, 0)

    def r1_add(s):
        arrived(("r1", s), r1.at[s])
        to_far, to_right, to_left = c * NX + far, c * NX + right, c * NX + left
        add_into(pb.at[s, to_far], r1.at[s, far], 0, cap)
        send(("ral", s), pb.at[s, to_far, low], ra.at[s, 0], dev_right)
        send(("rar", s), pb.at[s, to_far, high], ra.at[s, 1], dev_left)
        add_into(pb.at[s, to_right], r1.at[s, right], 0, cap)
        send(("rbl", s, 1), pb.at[s, to_right, high], rb.at[s, 0, high], dev_right)
        add_into(pb.at[s, to_left], r1.at[s, left], 0, cap)
        send(("rbr", s, 0), pb.at[s, to_left, low], rb.at[s, 1, low], dev_left)

    def ra_add(s):
        to_right, to_left = c * NX + right, c * NX + left
        arrived(("ral", s), ra.at[s, 0])
        add_into(pb.at[s, to_right], ra.at[s, 0], 0, half)
        send(("rbl", s, 0), pb.at[s, to_right, low], rb.at[s, 0, low], dev_right)
        arrived(("rar", s), ra.at[s, 1])
        add_into(pb.at[s, to_left], ra.at[s, 1], half, half)
        send(("rbr", s, 1), pb.at[s, to_left, high], rb.at[s, 1, high], dev_left)

    def combine(s):
        arrived(("rbl", s, 1), rb.at[s, 0, high])
        arrived(("rbr", s, 0), rb.at[s, 1, low])
        arrived(("rbl", s, 0), rb.at[s, 0, low])
        arrived(("rbr", s, 1), rb.at[s, 1, high])

        def final(i, carry):
            at = pl.ds(pl.multiple_of(i * piece, piece), piece)
            total = pb[s, c * NX + x, at].astype(jnp.float32) + r1[s, x, at].astype(jnp.float32)
            total += rb[s, 0, at].astype(jnp.float32) + rb[s, 1, at].astype(jnp.float32)
            total = total.astype(jnp.bfloat16)
            for q in range(NQ):
                to = pl.ds(pl.multiple_of(q * cap + i * piece, piece), piece)
                yb[to, :] = total[:, q * quarter:(q + 1) * quarter]
            return carry

        lax.fori_loop(0, cap // piece, final, 0)
        rows = nz * block

        def part(i, carry):
            first = pl.multiple_of(i * rows, rows)
            gain = jnp.where(slots_of(s, first, rows), gain_col[s, pl.ds(first, rows), 0:1], 0.0)
            coarse = gain.astype(jnp.bfloat16)
            fine = (gain - coarse.astype(jnp.float32)).astype(jnp.bfloat16)
            total = jnp.dot(coarse, yb[...], preferred_element_type=jnp.float32)
            total += jnp.dot(fine, yb[...], preferred_element_type=jnp.float32)
            db[s, pl.ds(i * nz, nz)] = total.astype(jnp.bfloat16).reshape(nz, block, quarter)
            return carry

        lax.fori_loop(0, ny, part, 0)
        for k in range(1, ny):
            send(("yr", s, k), db.at[s, pl.ds(((y + k) % ny) * nz, nz)], yr.at[s, k - 1], dev_y(k))

    def y_sum(s):
        for k in range(1, ny):
            arrived(("yr", s, k), yr.at[s, k - 1])

        def part(i, carry):
            total = db[s, y * nz + i].astype(jnp.float32)
            for k in range(1, ny):
                total += yr[s, k - 1, i].astype(jnp.float32)
            eb[s, i] = total.astype(jnp.bfloat16)
            return carry

        lax.fori_loop(0, nz, part, 0)
        for k in range(1, nz):
            send(("zr", s, k), eb.at[s, (z + k) % nz], zr.at[s, k - 1], dev_z(k))

    def z_sum(s):
        total = eb[s, z].astype(jnp.float32)
        for k in range(1, nz):
            arrived(("zr", s, k), zr.at[s, k - 1])
            total += zr[s, k - 1].astype(jnp.float32)
        out[s] = total.astype(jnp.bfloat16)

    route_z_send()
    for s in range(steps):
        z_send(s)
    earlier()
    route_y_send()
    for s in range(steps):
        z_wait(s)
        y_send(s)
    y_wait(0), select(0), x_own(0)
    x_near(0)
    y_wait(1), select(1), x_own(1)
    x_all(0)
    for load in loads:
        load.wait()
    experts(0)
    x_near(1)
    y_wait(2), select(2), x_own(2)
    r1_add(0)
    x_all(1)
    experts(1)
    ra_add(0)
    x_near(2)
    r1_add(1)
    x_all(2)
    experts(2)
    combine(0)
    ra_add(1)
    r1_add(2)
    y_sum(0)
    combine(1)
    ra_add(2)
    z_sum(0)
    y_sum(1)
    combine(2)
    z_sum(1)
    y_sum(2)
    z_sum(2)
    for copy in started:
        copy.wait_send()


def expert_copies(steps, ny, nz):
    return steps * (2 * (ny - 1) + 2 * (nz - 1) + 9 + 7) + ny + nz - 2


def expert_call(tokens, routes, top, w_gate, w_up, w_down, ny, nz):
    steps, block, quarter = tokens.shape
    cap = ny * nz * CAP_E
    width, hidden = w_gate.shape[1], w_gate.shape[2]
    copies = expert_copies(steps, ny, nz)
    bf16 = jnp.bfloat16
    any_spec = pl.BlockSpec(memory_space=pl.ANY)
    vmem_spec = pl.BlockSpec(memory_space=pltpu.VMEM)
    return pl.pallas_call(
        partial(expert_kernel, ny, nz, top),
        in_specs=[vmem_spec] * 2 + [any_spec] * 3,
        out_specs=vmem_spec,
        out_shape=jax.ShapeDtypeStruct(tokens.shape, bf16),
        scratch_shapes=[
            pltpu.VMEM((width, hidden), bf16),
            pltpu.VMEM((width, hidden), bf16),
            pltpu.VMEM((hidden, width), bf16),
            pltpu.VMEM((ny * nz,) + routes.shape, jnp.float32),
            pltpu.VMEM((ny * nz * block, ny * nz * block), bf16),
            pltpu.VMEM((steps, ny * nz * block, routes.shape[2]), jnp.float32),
            pltpu.VMEM((steps, ny * nz * block, routes.shape[2]), jnp.float32),
            pltpu.VMEM((steps, ny * nz, block, quarter), bf16),
            pltpu.VMEM((steps, 2 * NX, cap, width), bf16),
            pltpu.VMEM((steps, 2 * NX, cap, width), bf16),
            pltpu.VMEM((steps, NX, cap, width), bf16),
            pltpu.VMEM((steps, 2, cap // 2, width), bf16),
            pltpu.VMEM((steps, 2, cap, width), bf16),
            pltpu.VMEM((NQ * cap, quarter), bf16),
            pltpu.VMEM((steps, ny * nz, block, quarter), bf16),
            pltpu.VMEM((steps, max(ny - 1, 1), nz, block, quarter), bf16),
            pltpu.VMEM((steps, nz, block, quarter), bf16),
            pltpu.VMEM((steps, max(nz - 1, 1), block, quarter), bf16),
            pltpu.SemaphoreType.DMA((3,)),
            pltpu.SemaphoreType.DMA((copies,)),
            pltpu.SemaphoreType.DMA((copies,)),
        ],
        compiler_params=pltpu.CompilerParams(
            collective_id=0, has_side_effects=True, vmem_limit_bytes=60 << 20
        ),
    )(tokens, routes, w_gate, w_up, w_down)


def moe(moe_input, expert_ids, route_gains, w_gate, w_up, w_down, ny):
    group = lax.axis_index("grp")
    nz = lax.axis_size("ep") // ny
    steps, owned, width = moe_input.shape
    quarter = width // NQ
    own_ids = lax.dynamic_index_in_dim(expert_ids, group, 1, keepdims=False)
    own_gains = lax.dynamic_index_in_dim(route_gains, group, 1, keepdims=False)
    top = own_ids.shape[2]
    routes = jnp.concatenate([own_ids.astype(jnp.float32), own_gains], axis=2)
    routes = jnp.pad(routes, ((0, 0), (0, 0), (0, 128 - 2 * top)))
    routes = jnp.broadcast_to(routes[:, None], (steps, NQ, owned, 128)).reshape(steps, -1, 128)
    tokens = jnp.swapaxes(moe_input.reshape(steps, owned, NQ, quarter), 1, 2)
    tokens = tokens.reshape(steps, NQ * owned, quarter)
    out = expert_call(tokens, routes, top, w_gate, w_up, w_down, ny, nz)
    out = jnp.swapaxes(out.reshape(steps, NQ, owned, quarter), 1, 2)
    return out.reshape(steps, owned, width)


def migrate(grown, plan):
    group = lax.axis_index("grp")
    column = plan[:, 0]
    entries = column.shape[1]
    own = lax.dynamic_index_in_dim(column, group, 0, keepdims=False)
    outgoing = jnp.stack(
        [lax.dynamic_index_in_dim(grown, own[k, 0], 0, keepdims=False) for k in range(entries)]
    )
    received = lax.all_gather(outgoing, "grp", axis=0, tiled=True)
    result = grown
    for k in range(entries):
        source = jnp.sum(
            jnp.where(column[:, k, 1] == group, jnp.arange(column.shape[0], dtype=jnp.int32), 0)
        )
        incoming = lax.dynamic_index_in_dim(received, source * entries + k, 0, keepdims=True)
        result = lax.dynamic_update_slice(result, incoming, (own[k, 0], 0, 0))
    return result


def body(
    ny, queries, cache, new_entries, lengths, moe_input, expert_ids, route_gains,
    w_gate, w_up, w_down, plan,
):
    contexts, grown = attention(
        lengths, jnp.swapaxes(queries, 2, 3), jnp.swapaxes(cache, 1, 2), new_entries
    )
    moe_output = moe(moe_input, expert_ids, route_gains, w_gate, w_up, w_down, ny)
    migrated_cache = jnp.swapaxes(migrate(grown, plan), 1, 2)
    return (contexts, migrated_cache, moe_output)


def solution(mesh):
    return jax.shard_map(
        partial(body, NY),
        mesh=mesh,
        in_specs=(
            P(None, ("grp", "ep"), None, None),
            P(("grp", "ep"), None, None),
            P(None, ("grp", "ep"), None),
            P(("grp", "ep")),
            P(None, ("grp", "ep"), None),
            P(None, None, "ep", None),
            P(None, None, "ep", None),
            P("ep", None, "grp"),
            P("ep", None, "grp"),
            P("ep", "grp", None),
            P(None, "ep", None, None),
        ),
        out_specs=(
            P(None, ("grp", "ep"), None, None),
            P(("grp", "ep"), None, None),
            P(None, ("grp", "ep"), None),
        ),
        check_vma=False,
    )
```

```python
from functools import partial

import jax
import jax.numpy as jnp
from jax import lax
from jax.experimental import pallas as pl
from jax.experimental.pallas import tpu as pltpu
from jax.sharding import PartitionSpec as P

ROPE = 64
SCORE_SCALE = 192.0 ** (-0.5)
NX = 4
NY = 4
NQ = 4
CAP_E = 2
MESH = pl.DeviceIdType.MESH


def attention_kernel(lengths, queries, cache, entries, contexts, grown):
    filled = lengths[pl.program_id(0)]
    steps, latent = queries.shape[0], contexts.shape[3]
    rows = cache.shape[2]
    at_row = lax.broadcasted_iota(jnp.int32, (entries.shape[1], rows), 1) - filled
    step_of = lax.broadcasted_iota(jnp.int32, (entries.shape[1], rows), 0)
    place = jnp.where((at_row == step_of) & (step_of < steps), 1.0, 0.0).astype(jnp.bfloat16)
    added = lax.dot_general(
        entries[0], place, (((0,), (0,)), ((), ())), preferred_element_type=jnp.float32
    )
    lane = lax.broadcasted_iota(jnp.int32, (1, rows), 1) - filled
    old = cache[0].astype(jnp.float32)
    keys = jnp.where((lane >= 0) & (lane < steps), added, old)
    grown[0] = keys.astype(jnp.bfloat16)
    keys = keys.T.astype(jnp.bfloat16)
    position = lax.broadcasted_iota(jnp.int32, (rows, 1), 0) - filled
    for step in range(steps):
        scores = jnp.dot(keys, queries[step, 0], preferred_element_type=jnp.float32)
        scores = jnp.where(position <= step, scores * SCORE_SCALE, -jnp.inf)
        raised = jnp.exp(scores - jnp.max(scores, axis=0, keepdims=True))
        weights = raised / jnp.sum(raised, axis=0, keepdims=True)
        contexts[step, 0] = jnp.dot(
            weights.T.astype(jnp.bfloat16), keys[:, :latent], preferred_element_type=jnp.float32
        ).astype(jnp.bfloat16)


def attention(lengths, queries, cache, entries):
    steps, traces, width, heads = queries.shape
    rows, latent = cache.shape[2], width - ROPE
    entries = jnp.pad(jnp.swapaxes(entries, 0, 1), ((0, 0), (0, 16 - steps), (0, 0)))
    return pl.pallas_call(
        attention_kernel,
        grid_spec=pltpu.PrefetchScalarGridSpec(
            num_scalar_prefetch=1,
            grid=(traces,),
            in_specs=[
                pl.BlockSpec((steps, 1, width, heads), lambda t, n: (0, t, 0, 0)),
                pl.BlockSpec((1, width, rows), lambda t, n: (t, 0, 0)),
                pl.BlockSpec((1, 16, width), lambda t, n: (t, 0, 0)),
            ],
            out_specs=[
                pl.BlockSpec((steps, 1, heads, latent), lambda t, n: (0, t, 0, 0)),
                pl.BlockSpec((1, width, rows), lambda t, n: (t, 0, 0)),
            ],
        ),
        out_shape=[
            jax.ShapeDtypeStruct((steps, traces, heads, latent), jnp.bfloat16),
            jax.ShapeDtypeStruct(cache.shape, cache.dtype),
        ],
        compiler_params=pltpu.CompilerParams(vmem_limit_bytes=16 << 20),
        cost_estimate=pl.CostEstimate(
            flops=2 * steps * traces * heads * rows * (width + latent),
            bytes_accessed=8 << 20,
            transcendentals=steps * traces * heads * rows,
        ),
    )(lengths, queries, cache, entries)


def expert_kernel(
    ny, nz, top, source, tokens, routes, outgoing, wg_hbm, wu_hbm, wd_hbm, out, incoming,
    wg, wu, wd, mb, rt, tri, rank_col, gain_col, hb, tb, xb, pb, r1, ra, rb, yb, db, yr, eb, zr,
    wsem, send_sems, recv_sems,
):
    steps = tokens.shape[0]
    block, quarter = tokens.shape[1], tokens.shape[2]
    cap = xb.shape[2] // NQ
    group, expert = lax.axis_index("grp"), lax.axis_index("ep")
    x, c = group // 2, group % 2
    y, z = expert // nz, expert % nz
    right, left, far = (x + 1) % NX, (x + NX - 1) % NX, (x + 2) % NX
    dev_right, dev_left = (right * 2 + c, expert), (left * 2 + c, expert)
    dev_sib = (x * 2 + 1 - c, expert)

    def dev_y(k):
        return (group, ((y + k) % ny) * nz + z)

    def dev_z(k):
        return (group, y * nz + (z + k) % nz)

    peers = [dev_right, dev_left, dev_sib]
    peers += [dev_y(k) for k in range(1, ny)] + [dev_z(k) for k in range(1, nz)]
    barrier = pltpu.get_barrier_semaphore()
    for peer in peers:
        pl.semaphore_signal(barrier, inc=1, device_id=peer, device_id_type=MESH)
    loads = [
        pltpu.make_async_copy(hbm.at[0], vmem, wsem.at[i])
        for i, (hbm, vmem) in enumerate(((wg_hbm, wg), (wu_hbm, wu), (wd_hbm, wd)))
    ]
    for load in loads:
        load.start()
    pl.semaphore_wait(barrier, len(peers))

    number = {}
    started = []

    def slot(tag):
        return number.setdefault(tag, len(number))

    def send(tag, src, dst, dev):
        i = slot(tag)
        copy = pltpu.make_async_remote_copy(
            src_ref=src, dst_ref=dst, send_sem=send_sems.at[i], recv_sem=recv_sems.at[i],
            device_id=dev, device_id_type=MESH,
        )
        copy.start()
        started.append(copy)

    def arrived(tag, dst):
        i = slot(tag)
        pltpu.make_async_remote_copy(
            src_ref=dst, dst_ref=dst, send_sem=send_sems.at[i], recv_sem=recv_sems.at[i],
            device_id=dev_right, device_id_type=MESH,
        ).wait_recv()

    def route_z_send():
        rt[expert] = routes[...]
        for k in range(1, nz):
            send(("rz", k), rt.at[expert], rt.at[expert], dev_z(k))

    def route_y_send():
        for k in range(1, nz):
            arrived(("rz", k), rt.at[y * nz + (z + nz - k) % nz])
        part = rt.at[pl.ds(y * nz, nz)]
        for k in range(1, ny):
            send(("ry", k), part, part, dev_y(k))

    def z_send(s, p):
        for k in range(1, nz):
            part = tb.at[s, expert, :, p]
            send(("z", s, p.start, k), part, part, dev_z(k))

    def z_wait(s, p):
        for k in range(1, nz):
            arrived(("z", s, p.start, k), tb.at[s, y * nz + (z + nz - k) % nz, :, p])

    def y_send(s, p):
        part = tb.at[s, pl.ds(y * nz, nz), :, p]
        for k in range(1, ny):
            send(("y", s, p.start, k), part, part, dev_y(k))

    def y_wait(s, p):
        for k in range(1, ny):
            first = (y + ny - k) % ny * nz
            arrived(("y", s, p.start, k), tb.at[s, pl.ds(first, nz), :, p])

    columns = ny * nz * block
    owned = block // NQ

    def earlier():
        row = lax.broadcasted_iota(jnp.int32, (columns, columns), 0)
        other = lax.broadcasted_iota(jnp.int32, (columns, columns), 1)
        row_token = row // block * owned + row % owned
        other_token = other // block * owned + other % owned
        counted = ((other // owned) % NQ == 0) & (other_token < row_token)
        tri[...] = jnp.where(counted, 1.0, 0.0).astype(jnp.bfloat16)

    def rank(s):
        if s == 0:
            for k in range(1, ny):
                arrived(("ry", k), rt.at[pl.ds(((y + ny - k) % ny) * nz, nz)])
        route = rt[...].reshape(columns, rt.shape[2]).astype(jnp.float32)
        lane = lax.broadcasted_iota(jnp.int32, route.shape, 1) - 4 * top * s
        hit = (route == expert.astype(jnp.float32)) & (lane >= 0) & (lane < top)
        gains = sum(pltpu.roll(route, rt.shape[2] - k * top, 1) for k in (1, 2, 3))
        gain = jnp.sum(jnp.where(hit, gains, 0.0), axis=1, keepdims=True)
        chosen = jnp.sum(jnp.where(hit, 1.0, 0.0), axis=1, keepdims=True)
        chosen = jnp.broadcast_to(chosen, route.shape)
        before = jnp.dot(tri[...], chosen.astype(jnp.bfloat16), preferred_element_type=jnp.float32)
        rank_col[s] = jnp.where(chosen > 0.5, before, -1.0)
        gain_col[s] = jnp.broadcast_to(gain, route.shape)

    def slots_of(s, first, rows):
        at = pl.ds(first, rows)
        sub = lax.broadcasted_iota(jnp.int32, (rows, NQ * cap), 0)
        lane = lax.broadcasted_iota(jnp.int32, (rows, NQ * cap), 1)
        return (rank_col[s, at, 0:1] == (lane % cap).astype(jnp.float32)) & (
            (sub // owned) % NQ == lane // cap
        )

    def select(s, p):
        pick = jnp.where(slots_of(s, 0, columns), 1.0, 0.0).astype(jnp.bfloat16)
        rows = lax.dot_general(
            pick, tb[s, :, :, p].reshape(columns, p.stop - p.start), (((0,), (0,)), ((), ())),
            preferred_element_type=jnp.float32,
        )
        xb[s, c * NX + x, :, p] = rows.astype(jnp.bfloat16)

    half = NQ * cap // 2
    low, high = pl.ds(0, half), pl.ds(half, half)

    def x_own(s, p):
        mine = xb.at[s, c * NX + x, :, p]
        send(("xl", s, p.start), mine, mine, dev_right)
        send(("xr", s, p.start), mine, mine, dev_left)
        send(("so", s, p.start), mine, mine, dev_sib)

    def x_near(s, p):
        from_left, from_right = xb.at[s, c * NX + left], xb.at[s, c * NX + right]
        arrived(("xl", s, p.start), from_left.at[:, p])
        send(("x2l", s, p.start), from_left.at[low, p], from_left.at[low, p], dev_right)
        send(("sl", s, p.start), from_left.at[:, p], from_left.at[:, p], dev_sib)
        arrived(("xr", s, p.start), from_right.at[:, p])
        send(("x2r", s, p.start), from_right.at[high, p], from_right.at[high, p], dev_left)
        send(("sr", s, p.start), from_right.at[:, p], from_right.at[:, p], dev_sib)

    def x_all(s, p):
        across, other = xb.at[s, c * NX + far], (1 - c) * NX
        arrived(("x2l", s, p.start), across.at[low, p])
        send(("s2l", s, p.start), across.at[low, p], across.at[low, p], dev_sib)
        arrived(("x2r", s, p.start), across.at[high, p])
        send(("s2r", s, p.start), across.at[high, p], across.at[high, p], dev_sib)
        arrived(("so", s, p.start), xb.at[s, other + x, :, p])
        arrived(("sl", s, p.start), xb.at[s, other + left, :, p])
        arrived(("sr", s, p.start), xb.at[s, other + right, :, p])
        arrived(("s2l", s, p.start), xb.at[s, other + far, low, p])
        arrived(("s2r", s, p.start), xb.at[s, other + far, high, p])

    def experts(s):
        def part(h, carry):
            gate, up = 0.0, 0.0
            for q in range(NQ):
                rows = xb[s, pl.ds(h * NX, NX), q * cap:(q + 1) * cap, :]
                rows = rows.reshape(NX * cap, quarter)
                cols = slice(q * quarter, (q + 1) * quarter)
                gate += jnp.dot(rows, wg[cols, :], preferred_element_type=jnp.float32)
                up += jnp.dot(rows, wu[cols, :], preferred_element_type=jnp.float32)
            hb[h] = (gate / (1.0 + jnp.exp(-gate)) * up).astype(jnp.bfloat16)
            return carry

        lax.fori_loop(0, 2, part, 0)

    def outputs(s, p):
        def part(h, carry):
            for q in range(NQ):
                cols = slice(q * quarter + p.start, q * quarter + p.stop)
                pb[s, pl.ds(h * NX, NX), q * cap:(q + 1) * cap, p] = (
                    jnp.dot(hb[h], wd[:, cols], preferred_element_type=jnp.float32)
                    .astype(jnp.bfloat16).reshape(NX, cap, p.stop - p.start)
                )
            return carry

        lax.fori_loop(0, 2, part, 0)
        theirs = pb.at[s, pl.ds((1 - c) * NX, NX), :, p]
        send(("r1", s, p.start), theirs, r1.at[s, :, :, p], dev_sib)

    def m_own():
        mine = c * NX + x
        mb[mine] = outgoing[...]
        send("ml", mb.at[mine], mb.at[mine], dev_right)
        send("mr", mb.at[mine], mb.at[mine], dev_left)
        send("ms", mb.at[mine], mb.at[mine], dev_sib)

    def m_near():
        from_left, from_right = c * NX + left, c * NX + right
        arrived("ml", mb.at[from_left])
        send("m2l", mb.at[from_left, 0], mb.at[from_left, 0], dev_right)
        send("msl", mb.at[from_left], mb.at[from_left], dev_sib)
        arrived("mr", mb.at[from_right])
        send("m2r", mb.at[from_right, 1], mb.at[from_right, 1], dev_left)
        send("msr", mb.at[from_right], mb.at[from_right], dev_sib)

    def m_far():
        across = c * NX + far
        arrived("m2l", mb.at[across, 0])
        send("ms2l", mb.at[across, 0], mb.at[across, 0], dev_sib)
        arrived("m2r", mb.at[across, 1])
        send("ms2r", mb.at[across, 1], mb.at[across, 1], dev_sib)

    def m_take():
        other = (1 - c) * NX
        arrived("ms", mb.at[other + x])
        arrived("msl", mb.at[other + left])
        arrived("msr", mb.at[other + right])
        arrived("ms2l", mb.at[other + far, 0])
        arrived("ms2r", mb.at[other + far, 1])
        for k in range(incoming.shape[0]):
            incoming[k] = mb[source[k], k]

    piece = 32

    def add_into(dst, other, first, rows, p, shift=0):
        def part(i, carry):
            at = pl.ds(pl.multiple_of(first + i * piece, piece), piece)
            inner = pl.ds(pl.multiple_of(first - shift + i * piece, piece), piece)
            total = dst[at, p].astype(jnp.float32) + other[inner, p].astype(jnp.float32)
            dst[at, p] = total.astype(jnp.bfloat16)
            return carry

        lax.fori_loop(0, rows // piece, part, 0)

    def r1_add(s, p):
        arrived(("r1", s, p.start), r1.at[s, :, :, p])
        to_far, to_right, to_left = c * NX + far, c * NX + right, c * NX + left
        add_into(pb.at[s, to_far], r1.at[s, far], 0, 2 * half, p)
        send(("ral", s, p.start), pb.at[s, to_far, low, p], ra.at[s, 0, :, p], dev_right)
        send(("rar", s, p.start), pb.at[s, to_far, high, p], ra.at[s, 1, :, p], dev_left)
        add_into(pb.at[s, to_right], r1.at[s, right], 0, 2 * half, p)
        send(("rbl", s, p.start, 1), pb.at[s, to_right, high, p], rb.at[s, 0, high, p], dev_right)
        add_into(pb.at[s, to_left], r1.at[s, left], 0, 2 * half, p)
        send(("rbr", s, p.start, 0), pb.at[s, to_left, low, p], rb.at[s, 1, low, p], dev_left)

    def ra_add(s, p):
        to_right, to_left = c * NX + right, c * NX + left
        arrived(("ral", s, p.start), ra.at[s, 0, :, p])
        add_into(pb.at[s, to_right], ra.at[s, 0], 0, half, p)
        send(("rbl", s, p.start, 0), pb.at[s, to_right, low, p], rb.at[s, 0, low, p], dev_right)
        arrived(("rar", s, p.start), ra.at[s, 1, :, p])
        add_into(pb.at[s, to_left], ra.at[s, 1], half, half, p, half)
        send(("rbr", s, p.start, 1), pb.at[s, to_left, high, p], rb.at[s, 1, high, p], dev_left)

    def combine(s, p):
        arrived(("rbl", s, p.start, 1), rb.at[s, 0, high, p])
        arrived(("rbr", s, p.start, 0), rb.at[s, 1, low, p])
        arrived(("rbl", s, p.start, 0), rb.at[s, 0, low, p])
        arrived(("rbr", s, p.start, 1), rb.at[s, 1, high, p])

        def final(i, carry):
            at = pl.ds(pl.multiple_of(i * piece, piece), piece)
            total = pb[s, c * NX + x, at, p].astype(jnp.float32)
            total += r1[s, x, at, p].astype(jnp.float32)
            total += rb[s, 0, at, p].astype(jnp.float32) + rb[s, 1, at, p].astype(jnp.float32)
            yb[at, p] = total.astype(jnp.bfloat16)
            return carry

        lax.fori_loop(0, NQ * cap // piece, final, 0)
        rows = nz * block

        def part(i, carry):
            first = pl.multiple_of(i * rows, rows)
            gain = jnp.where(slots_of(s, first, rows), gain_col[s, pl.ds(first, rows), 0:1], 0.0)
            coarse = gain.astype(jnp.bfloat16)
            fine = (gain - coarse.astype(jnp.float32)).astype(jnp.bfloat16)
            total = jnp.dot(coarse, yb[:, p], preferred_element_type=jnp.float32)
            total += jnp.dot(fine, yb[:, p], preferred_element_type=jnp.float32)
            db[s, pl.ds(i * nz, nz), :, p] = (
                total.astype(jnp.bfloat16).reshape(nz, block, p.stop - p.start)
            )
            return carry

        lax.fori_loop(0, ny, part, 0)
        for k in range(1, ny):
            theirs = db.at[s, pl.ds((y + k) % ny * nz, nz), :, p]
            send(("yr", s, p.start, k), theirs, yr.at[s, k - 1, :, :, p], dev_y(k))

    def y_sum(s, p):
        for k in range(1, ny):
            arrived(("yr", s, p.start, k), yr.at[s, k - 1, :, :, p])

        def part(i, carry):
            total = db[s, y * nz + i, :, p].astype(jnp.float32)
            for k in range(1, ny):
                total += yr[s, k - 1, i, :, p].astype(jnp.float32)
            eb[s, i, :, p] = total.astype(jnp.bfloat16)
            return carry

        lax.fori_loop(0, nz, part, 0)
        for k in range(1, nz):
            theirs = eb.at[s, (z + k) % nz, :, p]
            send(("zr", s, p.start, k), theirs, zr.at[s, k - 1, :, p], dev_z(k))

    def z_sum(s, p):
        total = eb[s, z, :, p].astype(jnp.float32)
        for k in range(1, nz):
            arrived(("zr", s, p.start, k), zr.at[s, k - 1, :, p])
            total += zr[s, k - 1, :, p].astype(jnp.float32)
        out[s, :, p] = total.astype(jnp.bfloat16)

    whole = slice(0, quarter)
    a, b = quarter // 384 * 128, quarter // 384 * 256
    pieces = [slice(0, a), slice(a, b), slice(b, quarter)]

    route_z_send()
    for s in range(steps):
        tb[s, expert] = tokens[s]
    for p in pieces:
        z_send(0, p)
    earlier()
    route_y_send()
    for p in pieces:
        z_wait(0, p), y_send(0, p)
    z_send(1, whole)
    for p in pieces:
        y_wait(0, p)
        if p is pieces[0]:
            rank(0)
        select(0, p), x_own(0, p)
    z_wait(1, whole), y_send(1, whole), z_send(2, whole)
    rank(1), rank(2)
    for p in pieces:
        x_near(0, p)
    y_wait(1, whole), select(1, whole), x_own(1, whole)
    z_wait(2, whole), y_send(2, whole)
    for p in pieces:
        x_all(0, p)
    for load in loads:
        load.wait()
    experts(0), outputs(0, whole)
    x_near(1, whole)
    y_wait(2, whole), select(2, whole), x_own(2, whole)
    r1_add(0, whole)
    x_all(1, whole)
    experts(1), outputs(1, whole)
    ra_add(0, whole)
    x_near(2, whole)
    r1_add(1, whole)
    x_all(2, whole)
    experts(2)
    for p in pieces:
        outputs(2, p)
    combine(0, whole)
    ra_add(1, whole)
    for p in pieces:
        r1_add(2, p)
    y_sum(0, whole)
    combine(1, whole)
    for p in pieces:
        ra_add(2, p)
    m_own()
    z_sum(0, whole)
    y_sum(1, whole)
    for p in pieces:
        combine(2, p)
    z_sum(1, whole)
    m_near()
    for p in pieces:
        y_sum(2, p)
    m_far()
    for p in pieces:
        z_sum(2, p)
    m_take()
    for copy in started:
        copy.wait_send()


def expert_copies(steps, ny, nz):
    return (steps + 2) * (2 * (ny - 1) + 2 * (nz - 1) + 9 + 7) + ny + nz - 2 + 9


def expert_call(source, tokens, routes, top, outgoing, w_gate, w_up, w_down, ny, nz):
    steps, block, quarter = tokens.shape
    cap = ny * nz * CAP_E
    width, hidden = w_gate.shape[1], w_gate.shape[2]
    copies = expert_copies(steps, ny, nz)
    bf16 = jnp.bfloat16
    any_spec = pl.BlockSpec(memory_space=pl.ANY)
    vmem_spec = pl.BlockSpec(memory_space=pltpu.VMEM)
    return pl.pallas_call(
        partial(expert_kernel, ny, nz, top),
        in_specs=[pl.BlockSpec(memory_space=pltpu.SMEM)] + [vmem_spec] * 3 + [any_spec] * 3,
        out_specs=[vmem_spec] * 2,
        out_shape=[
            jax.ShapeDtypeStruct(tokens.shape, bf16),
            jax.ShapeDtypeStruct(outgoing.shape, bf16),
        ],
        scratch_shapes=[
            pltpu.VMEM((width, hidden), bf16),
            pltpu.VMEM((width, hidden), bf16),
            pltpu.VMEM((hidden, width), bf16),
            pltpu.VMEM((2 * NX,) + outgoing.shape, bf16),
            pltpu.VMEM((ny * nz,) + routes.shape, bf16),
            pltpu.VMEM((ny * nz * block, ny * nz * block), bf16),
            pltpu.VMEM((steps, ny * nz * block, routes.shape[1]), jnp.float32),
            pltpu.VMEM((steps, ny * nz * block, routes.shape[1]), jnp.float32),
            pltpu.VMEM((2, NX * cap, hidden), bf16),
            pltpu.VMEM((steps, ny * nz, block, quarter), bf16),
            pltpu.VMEM((steps, 2 * NX, NQ * cap, quarter), bf16),
            pltpu.VMEM((steps, 2 * NX, NQ * cap, quarter), bf16),
            pltpu.VMEM((steps, NX, NQ * cap, quarter), bf16),
            pltpu.VMEM((steps, 2, NQ * cap // 2, quarter), bf16),
            pltpu.VMEM((steps, 2, NQ * cap, quarter), bf16),
            pltpu.VMEM((NQ * cap, quarter), bf16),
            pltpu.VMEM((steps, ny * nz, block, quarter), bf16),
            pltpu.VMEM((steps, max(ny - 1, 1), nz, block, quarter), bf16),
            pltpu.VMEM((steps, nz, block, quarter), bf16),
            pltpu.VMEM((steps, max(nz - 1, 1), block, quarter), bf16),
            pltpu.SemaphoreType.DMA((3,)),
            pltpu.SemaphoreType.DMA((copies,)),
            pltpu.SemaphoreType.DMA((copies,)),
        ],
        compiler_params=pltpu.CompilerParams(
            collective_id=0, has_side_effects=True, vmem_limit_bytes=60 << 20
        ),
    )(source, tokens, routes, outgoing, w_gate, w_up, w_down)


def narrow(value):
    return lax.reduce_precision(value, exponent_bits=8, mantissa_bits=7)


def body(
    ny, queries, cache, new_entries, lengths, moe_input, expert_ids, route_gains,
    w_gate, w_up, w_down, plan,
):
    contexts, grown = attention(
        lengths, jnp.swapaxes(queries, 2, 3), jnp.swapaxes(cache, 1, 2), new_entries
    )
    group = lax.axis_index("grp")
    nz = lax.axis_size("ep") // ny

    column = plan[:, 0]
    entries = column.shape[1]
    own = lax.dynamic_index_in_dim(column, group, 0, keepdims=False)
    outgoing = jnp.stack(
        [lax.dynamic_index_in_dim(grown, own[k, 0], 0, keepdims=False) for k in range(entries)]
    )
    senders = jnp.arange(column.shape[0], dtype=jnp.int32)
    places = senders % 2 * NX + senders // 2
    source = jnp.sum(jnp.where(column[:, :, 1] == group, places[:, None], 0), axis=0)

    steps, owned, width = moe_input.shape
    quarter = width // NQ
    own_ids = lax.dynamic_index_in_dim(expert_ids, group, 1, keepdims=False)
    gains = lax.dynamic_index_in_dim(route_gains, group, 1, keepdims=False)
    top = own_ids.shape[2]
    first = narrow(gains)
    second = narrow(gains - first)
    third = gains - first - second
    routes = jnp.concatenate([own_ids.astype(jnp.float32), first, second, third], axis=2)
    routes = jnp.swapaxes(routes.astype(jnp.bfloat16), 0, 1).reshape(owned, -1)
    routes = jnp.pad(routes, ((0, 0), (0, 128 - routes.shape[1])))
    routes = jnp.broadcast_to(routes[None], (NQ, owned, 128)).reshape(-1, 128)
    tokens = jnp.swapaxes(moe_input.reshape(steps, owned, NQ, quarter), 1, 2)
    tokens = tokens.reshape(steps, NQ * owned, quarter)
    out, incoming = expert_call(
        source, tokens, routes, top, outgoing, w_gate, w_up, w_down, ny, nz
    )
    out = jnp.swapaxes(out.reshape(steps, NQ, owned, quarter), 1, 2)

    migrated = grown
    for k in range(entries):
        migrated = lax.dynamic_update_slice(migrated, incoming[k:k + 1], (own[k, 0], 0, 0))
    return (contexts, jnp.swapaxes(migrated, 1, 2), out.reshape(steps, owned, width))


def solution(mesh):
    return jax.shard_map(
        partial(body, NY),
        mesh=mesh,
        in_specs=(
            P(None, ("grp", "ep"), None, None),
            P(("grp", "ep"), None, None),
            P(None, ("grp", "ep"), None),
            P(("grp", "ep")),
            P(None, ("grp", "ep"), None),
            P(None, None, "ep", None),
            P(None, None, "ep", None),
            P("ep", None, "grp"),
            P("ep", None, "grp"),
            P("ep", "grp", None),
            P(None, "ep", None, None),
        ),
        out_specs=(
            P(None, ("grp", "ep"), None, None),
            P(("grp", "ep"), None, None),
            P(None, ("grp", "ep"), None),
        ),
        check_vma=False,
    )
```

```python
from functools import partial

import jax
import jax.numpy as jnp
from jax import lax
from jax.experimental import pallas as pl
from jax.experimental.pallas import tpu as pltpu
from jax.sharding import PartitionSpec as P

ROPE = 64
SCORE_SCALE = 192.0 ** (-0.5)
NX = 4
NY = 4
NQ = 4
CAP_E = 2
MESH = pl.DeviceIdType.MESH


def layer_kernel(
    ny, nz, top, plan, lengths, tokens, routes, entries, queries_hbm, cache_hbm, wg_hbm, wu_hbm, wd_hbm,
    out, migrated, contexts_hbm, wg, wu, wd, queries, cache, contexts, mb, rt, tri, rank_col, gain_col, hb, tb, xb, pb, r1, ra, rb, yb, db, yr, eb, zr,
    wsem, send_sems, recv_sems,
):
    steps, owned = tokens.shape[0], tokens.shape[1]
    block, quarter = NQ * owned, tokens.shape[2] // NQ
    cap = xb.shape[2] // NQ
    group, expert = lax.axis_index("grp"), lax.axis_index("ep")
    x, c = group // 2, group % 2
    y, z = expert // nz, expert % nz
    right, left, far = (x + 1) % NX, (x + NX - 1) % NX, (x + 2) % NX
    dev_right, dev_left = (right * 2 + c, expert), (left * 2 + c, expert)
    dev_sib = (x * 2 + 1 - c, expert)

    def dev_y(k):
        return (group, ((y + k) % ny) * nz + z)

    def dev_z(k):
        return (group, y * nz + (z + k) % nz)

    peers = [dev_right, dev_left, dev_sib]
    peers += [dev_y(k) for k in range(1, ny)] + [dev_z(k) for k in range(1, nz)]
    barrier = pltpu.get_barrier_semaphore()
    for peer in peers:
        pl.semaphore_signal(barrier, inc=1, device_id=peer, device_id_type=MESH)
    cache_load = pltpu.make_async_copy(cache_hbm, cache, wsem.at[3])
    query_load = pltpu.make_async_copy(queries_hbm, queries, wsem.at[4])
    context_store = pltpu.make_async_copy(contexts, contexts_hbm, wsem.at[5])
    loads = [
        pltpu.make_async_copy(hbm.at[0], vmem, wsem.at[i])
        for i, (hbm, vmem) in enumerate(((wg_hbm, wg), (wu_hbm, wu), (wd_hbm, wd)))
    ]
    for load in [cache_load, query_load] + loads:
        load.start()
    pl.semaphore_wait(barrier, len(peers))

    number = {}
    started = []

    def slot(tag):
        return number.setdefault(tag, len(number))

    def send(tag, src, dst, dev):
        i = slot(tag)
        copy = pltpu.make_async_remote_copy(
            src_ref=src, dst_ref=dst, send_sem=send_sems.at[i], recv_sem=recv_sems.at[i],
            device_id=dev, device_id_type=MESH,
        )
        copy.start()
        started.append(copy)

    def arrived(tag, dst):
        i = slot(tag)
        pltpu.make_async_remote_copy(
            src_ref=dst, dst_ref=dst, send_sem=send_sems.at[i], recv_sem=recv_sems.at[i],
            device_id=dev_right, device_id_type=MESH,
        ).wait_recv()

    def route_z_send():
        rt[expert] = routes[...]
        for k in range(1, nz):
            send(("rz", k), rt.at[expert], rt.at[expert], dev_z(k))

    def route_y_send():
        for k in range(1, nz):
            arrived(("rz", k), rt.at[y * nz + (z + nz - k) % nz])
        part = rt.at[pl.ds(y * nz, nz)]
        for k in range(1, ny):
            send(("ry", k), part, part, dev_y(k))

    def z_send(s, p):
        for k in range(1, nz):
            part = tb.at[s, expert, :, p]
            send(("z", s, p.start, k), part, part, dev_z(k))

    def z_wait(s, p):
        for k in range(1, nz):
            arrived(("z", s, p.start, k), tb.at[s, y * nz + (z + nz - k) % nz, :, p])

    def y_send(s, p):
        part = tb.at[s, pl.ds(y * nz, nz), :, p]
        for k in range(1, ny):
            send(("y", s, p.start, k), part, part, dev_y(k))

    def y_wait(s, p):
        for k in range(1, ny):
            first = (y + ny - k) % ny * nz
            arrived(("y", s, p.start, k), tb.at[s, pl.ds(first, nz), :, p])

    columns = ny * nz * block

    def earlier():
        row = lax.broadcasted_iota(jnp.int32, (columns, columns), 0)
        other = lax.broadcasted_iota(jnp.int32, (columns, columns), 1)
        row_token = row // block * owned + row % owned
        other_token = other // block * owned + other % owned
        counted = ((other // owned) % NQ == 0) & (other_token < row_token)
        tri[...] = jnp.where(counted, 1.0, 0.0).astype(jnp.bfloat16)

    def rank(s):
        if s == 0:
            for k in range(1, ny):
                arrived(("ry", k), rt.at[pl.ds(((y + ny - k) % ny) * nz, nz)])
        route = rt[...].reshape(columns, rt.shape[2]).astype(jnp.float32)
        lane = lax.broadcasted_iota(jnp.int32, route.shape, 1) - 4 * top * s
        hit = (route == expert.astype(jnp.float32)) & (lane >= 0) & (lane < top)
        gains = sum(pltpu.roll(route, rt.shape[2] - k * top, 1) for k in (1, 2, 3))
        gain = jnp.sum(jnp.where(hit, gains, 0.0), axis=1, keepdims=True)
        chosen = jnp.sum(jnp.where(hit, 1.0, 0.0), axis=1, keepdims=True)
        chosen = jnp.broadcast_to(chosen, route.shape)
        before = jnp.dot(tri[...], chosen.astype(jnp.bfloat16), preferred_element_type=jnp.float32)
        rank_col[s] = jnp.where(chosen > 0.5, before, -1.0)
        gain_col[s] = jnp.broadcast_to(gain, route.shape)

    def slots_of(s, first, rows):
        at = pl.ds(first, rows)
        sub = lax.broadcasted_iota(jnp.int32, (rows, NQ * cap), 0)
        lane = lax.broadcasted_iota(jnp.int32, (rows, NQ * cap), 1)
        return (rank_col[s, at, 0:1] == (lane % cap).astype(jnp.float32)) & (
            (sub // owned) % NQ == lane // cap
        )

    def select(s, p):
        pick = jnp.where(slots_of(s, 0, columns), 1.0, 0.0).astype(jnp.bfloat16)
        rows = lax.dot_general(
            pick, tb[s, :, :, p].reshape(columns, p.stop - p.start), (((0,), (0,)), ((), ())),
            preferred_element_type=jnp.float32,
        )
        xb[s, c * NX + x, :, p] = rows.astype(jnp.bfloat16)

    half = NQ * cap // 2
    low, high = pl.ds(0, half), pl.ds(half, half)

    def x_own(s, p):
        mine = xb.at[s, c * NX + x, :, p]
        send(("xl", s, p.start), mine, mine, dev_right)
        send(("xr", s, p.start), mine, mine, dev_left)
        send(("so", s, p.start), mine, mine, dev_sib)

    def x_near(s, p):
        from_left, from_right = xb.at[s, c * NX + left], xb.at[s, c * NX + right]
        arrived(("xl", s, p.start), from_left.at[:, p])
        send(("x2l", s, p.start), from_left.at[low, p], from_left.at[low, p], dev_right)
        send(("sl", s, p.start), from_left.at[:, p], from_left.at[:, p], dev_sib)
        arrived(("xr", s, p.start), from_right.at[:, p])
        send(("x2r", s, p.start), from_right.at[high, p], from_right.at[high, p], dev_left)
        send(("sr", s, p.start), from_right.at[:, p], from_right.at[:, p], dev_sib)

    def x_all(s, p):
        across, other = xb.at[s, c * NX + far], (1 - c) * NX
        arrived(("x2l", s, p.start), across.at[low, p])
        send(("s2l", s, p.start), across.at[low, p], across.at[low, p], dev_sib)
        arrived(("x2r", s, p.start), across.at[high, p])
        send(("s2r", s, p.start), across.at[high, p], across.at[high, p], dev_sib)
        arrived(("so", s, p.start), xb.at[s, other + x, :, p])
        arrived(("sl", s, p.start), xb.at[s, other + left, :, p])
        arrived(("sr", s, p.start), xb.at[s, other + right, :, p])
        arrived(("s2l", s, p.start), xb.at[s, other + far, low, p])
        arrived(("s2r", s, p.start), xb.at[s, other + far, high, p])

    def experts(s):
        def part(h, carry):
            gate, up = 0.0, 0.0
            for q in range(NQ):
                rows = xb[s, pl.ds(h * NX, NX), q * cap:(q + 1) * cap, :]
                rows = rows.reshape(NX * cap, quarter)
                cols = slice(q * quarter, (q + 1) * quarter)
                gate += jnp.dot(rows, wg[cols, :], preferred_element_type=jnp.float32)
                up += jnp.dot(rows, wu[cols, :], preferred_element_type=jnp.float32)
            hb[h] = (gate / (1.0 + jnp.exp(-gate)) * up).astype(jnp.bfloat16)
            return carry

        lax.fori_loop(0, 2, part, 0)

    def outputs(s, p):
        def part(h, carry):
            for q in range(NQ):
                cols = slice(q * quarter + p.start, q * quarter + p.stop)
                pb[s, pl.ds(h * NX, NX), q * cap:(q + 1) * cap, p] = (
                    jnp.dot(hb[h], wd[:, cols], preferred_element_type=jnp.float32)
                    .astype(jnp.bfloat16).reshape(NX, cap, p.stop - p.start)
                )
            return carry

        lax.fori_loop(0, 2, part, 0)
        theirs = pb.at[s, pl.ds((1 - c) * NX, NX), :, p]
        send(("r1", s, p.start), theirs, r1.at[s, :, :, p], dev_sib)

    def attend(t):
        filled = lengths[t]
        rows, latent = cache.shape[2], contexts.shape[3]
        at_row = lax.broadcasted_iota(jnp.int32, (entries.shape[1], rows), 1) - filled
        step_of = lax.broadcasted_iota(jnp.int32, (entries.shape[1], rows), 0)
        place = jnp.where((at_row == step_of) & (step_of < steps), 1.0, 0.0).astype(jnp.bfloat16)
        added = lax.dot_general(
            entries[t], place, (((0,), (0,)), ((), ())), preferred_element_type=jnp.float32
        )
        lane = lax.broadcasted_iota(jnp.int32, (1, rows), 1) - filled
        old = cache[t].astype(jnp.float32)
        keys = jnp.where((lane >= 0) & (lane < steps), added, old)
        cache[t] = keys.astype(jnp.bfloat16)
        keys = keys.T.astype(jnp.bfloat16)
        position = lax.broadcasted_iota(jnp.int32, (rows, 1), 0) - filled
        for step in range(steps):
            scores = jnp.dot(keys, queries[step, t], preferred_element_type=jnp.float32)
            scores = jnp.where(position <= step, scores * SCORE_SCALE, -jnp.inf)
            raised = jnp.exp(scores - jnp.max(scores, axis=0, keepdims=True))
            weights = raised / jnp.sum(raised, axis=0, keepdims=True)
            contexts[step, t] = jnp.dot(
                weights.T.astype(jnp.bfloat16), keys[:, :latent],
                preferred_element_type=jnp.float32,
            ).astype(jnp.bfloat16)

    def m_own():
        mine = c * NX + x
        for k in range(mb.shape[1]):
            mb[mine, k] = cache[plan[(group * mb.shape[1] + k) * 2]]
        send("ml", mb.at[mine], mb.at[mine], dev_right)
        send("mr", mb.at[mine], mb.at[mine], dev_left)
        send("ms", mb.at[mine], mb.at[mine], dev_sib)

    def m_near():
        from_left, from_right = c * NX + left, c * NX + right
        arrived("ml", mb.at[from_left])
        send("m2l", mb.at[from_left, 0], mb.at[from_left, 0], dev_right)
        send("msl", mb.at[from_left], mb.at[from_left], dev_sib)
        arrived("mr", mb.at[from_right])
        send("m2r", mb.at[from_right, 1], mb.at[from_right, 1], dev_left)
        send("msr", mb.at[from_right], mb.at[from_right], dev_sib)

    def m_far():
        across = c * NX + far
        arrived("m2l", mb.at[across, 0])
        send("ms2l", mb.at[across, 0], mb.at[across, 0], dev_sib)
        arrived("m2r", mb.at[across, 1])
        send("ms2r", mb.at[across, 1], mb.at[across, 1], dev_sib)

    def m_take():
        other = (1 - c) * NX
        arrived("ms", mb.at[other + x])
        arrived("msl", mb.at[other + left])
        arrived("msr", mb.at[other + right])
        arrived("ms2l", mb.at[other + far, 0])
        arrived("ms2r", mb.at[other + far, 1])
        entries_sent = mb.shape[1]
        lands, coming = [], []
        for k in range(entries_sent):
            sender = jnp.int32(0)
            for g in range(2 * NX):
                goes = plan[(g * entries_sent + k) * 2 + 1]
                sender = jnp.where(goes == group, g % 2 * NX + g // 2, sender)
            coming.append(sender)
            lands.append(plan[(group * entries_sent + k) * 2])

        def place(t, carry):
            value = cache[t].astype(jnp.float32)
            for k in range(entries_sent):
                here = jnp.broadcast_to(lands[k] - t, value.shape) == 0
                value = jnp.where(here, mb[coming[k], k].astype(jnp.float32), value)
            migrated[t] = value.astype(jnp.bfloat16)
            return carry

        lax.fori_loop(0, cache.shape[0], place, 0)

    piece = 32

    def add_into(dst, other, first, rows, p, shift=0):
        def part(i, carry):
            at = pl.ds(pl.multiple_of(first + i * piece, piece), piece)
            inner = pl.ds(pl.multiple_of(first - shift + i * piece, piece), piece)
            total = dst[at, p].astype(jnp.float32) + other[inner, p].astype(jnp.float32)
            dst[at, p] = total.astype(jnp.bfloat16)
            return carry

        lax.fori_loop(0, rows // piece, part, 0)

    def r1_add(s, p):
        arrived(("r1", s, p.start), r1.at[s, :, :, p])
        to_far, to_right, to_left = c * NX + far, c * NX + right, c * NX + left
        add_into(pb.at[s, to_far], r1.at[s, far], 0, 2 * half, p)
        send(("ral", s, p.start), pb.at[s, to_far, low, p], ra.at[s, 0, :, p], dev_right)
        send(("rar", s, p.start), pb.at[s, to_far, high, p], ra.at[s, 1, :, p], dev_left)
        add_into(pb.at[s, to_right], r1.at[s, right], 0, 2 * half, p)
        send(("rbl", s, p.start, 1), pb.at[s, to_right, high, p], rb.at[s, 0, high, p], dev_right)
        add_into(pb.at[s, to_left], r1.at[s, left], 0, 2 * half, p)
        send(("rbr", s, p.start, 0), pb.at[s, to_left, low, p], rb.at[s, 1, low, p], dev_left)

    def ra_add(s, p):
        to_right, to_left = c * NX + right, c * NX + left
        arrived(("ral", s, p.start), ra.at[s, 0, :, p])
        add_into(pb.at[s, to_right], ra.at[s, 0], 0, half, p)
        send(("rbl", s, p.start, 0), pb.at[s, to_right, low, p], rb.at[s, 0, low, p], dev_right)
        arrived(("rar", s, p.start), ra.at[s, 1, :, p])
        add_into(pb.at[s, to_left], ra.at[s, 1], half, half, p, half)
        send(("rbr", s, p.start, 1), pb.at[s, to_left, high, p], rb.at[s, 1, high, p], dev_left)

    def combine(s, p):
        arrived(("rbl", s, p.start, 1), rb.at[s, 0, high, p])
        arrived(("rbr", s, p.start, 0), rb.at[s, 1, low, p])
        arrived(("rbl", s, p.start, 0), rb.at[s, 0, low, p])
        arrived(("rbr", s, p.start, 1), rb.at[s, 1, high, p])

        def final(i, carry):
            at = pl.ds(pl.multiple_of(i * piece, piece), piece)
            total = pb[s, c * NX + x, at, p].astype(jnp.float32)
            total += r1[s, x, at, p].astype(jnp.float32)
            total += rb[s, 0, at, p].astype(jnp.float32) + rb[s, 1, at, p].astype(jnp.float32)
            yb[at, p] = total.astype(jnp.bfloat16)
            return carry

        lax.fori_loop(0, NQ * cap // piece, final, 0)
        rows = nz * block

        def part(i, carry):
            first = pl.multiple_of(i * rows, rows)
            gain = jnp.where(slots_of(s, first, rows), gain_col[s, pl.ds(first, rows), 0:1], 0.0)
            coarse = gain.astype(jnp.bfloat16)
            fine = (gain - coarse.astype(jnp.float32)).astype(jnp.bfloat16)
            total = jnp.dot(coarse, yb[:, p], preferred_element_type=jnp.float32)
            total += jnp.dot(fine, yb[:, p], preferred_element_type=jnp.float32)
            db[s, pl.ds(i * nz, nz), :, p] = (
                total.astype(jnp.bfloat16).reshape(nz, block, p.stop - p.start)
            )
            return carry

        lax.fori_loop(0, ny, part, 0)
        for k in range(1, ny):
            theirs = db.at[s, pl.ds((y + k) % ny * nz, nz), :, p]
            send(("yr", s, p.start, k), theirs, yr.at[s, k - 1, :, :, p], dev_y(k))

    def y_sum(s, p):
        for k in range(1, ny):
            arrived(("yr", s, p.start, k), yr.at[s, k - 1, :, :, p])

        def part(i, carry):
            total = db[s, y * nz + i, :, p].astype(jnp.float32)
            for k in range(1, ny):
                total += yr[s, k - 1, i, :, p].astype(jnp.float32)
            eb[s, i, :, p] = total.astype(jnp.bfloat16)
            return carry

        lax.fori_loop(0, nz, part, 0)
        for k in range(1, nz):
            theirs = eb.at[s, (z + k) % nz, :, p]
            send(("zr", s, p.start, k), theirs, zr.at[s, k - 1, :, p], dev_z(k))

    def z_sum(s, p):
        total = eb[s, z, :, p].astype(jnp.float32)
        for k in range(1, nz):
            arrived(("zr", s, p.start, k), zr.at[s, k - 1, :, p])
            total += zr[s, k - 1, :, p].astype(jnp.float32)
        for q in range(NQ):
            cols = slice(q * quarter + p.start, q * quarter + p.stop)
            out[s, :, cols] = total[q * owned:(q + 1) * owned].astype(jnp.bfloat16)

    whole = slice(0, quarter)
    a, b = quarter // 384 * 128, quarter // 384 * 256
    pieces = [slice(0, a), slice(a, b), slice(b, quarter)]

    route_z_send()
    for s in range(steps):
        row = tokens[s].astype(jnp.float32)
        row = [row[:, q * quarter:(q + 1) * quarter] for q in range(NQ)]
        tb[s, expert] = jnp.concatenate(row, axis=0).astype(jnp.bfloat16)
    for p in pieces:
        z_send(0, p)
    earlier()
    route_y_send()
    for p in pieces:
        z_wait(0, p), y_send(0, p)
    z_send(1, whole)
    for p in pieces:
        y_wait(0, p)
        if p is pieces[0]:
            rank(0)
        select(0, p), x_own(0, p)
    z_wait(1, whole), y_send(1, whole), z_send(2, whole)
    rank(1), rank(2)
    cache_load.wait(), query_load.wait()
    attend(0)
    for p in pieces:
        x_near(0, p)
    y_wait(1, whole), select(1, whole), x_own(1, whole)
    z_wait(2, whole), y_send(2, whole)
    for p in pieces:
        x_all(0, p)
    for load in loads:
        load.wait()
    experts(0), outputs(0, whole)
    attend(1)
    x_near(1, whole)
    y_wait(2, whole), select(2, whole), x_own(2, whole)
    r1_add(0, whole)
    x_all(1, whole)
    experts(1), outputs(1, whole)
    ra_add(0, whole)
    attend(2)
    x_near(2, whole)
    r1_add(1, whole)
    attend(3)
    context_store.start()
    x_all(2, whole)
    experts(2)
    for p in pieces:
        outputs(2, p)
    combine(0, whole)
    ra_add(1, whole)
    for p in pieces:
        r1_add(2, p)
    y_sum(0, whole)
    combine(1, whole)
    for p in pieces:
        ra_add(2, p)
    m_own()
    z_sum(0, whole)
    y_sum(1, whole)
    for p in pieces:
        combine(2, p)
    z_sum(1, whole)
    m_near()
    for p in pieces:
        y_sum(2, p)
    m_far()
    for p in pieces:
        z_sum(2, p)
    m_take()
    context_store.wait()
    for copy in started:
        copy.wait_send()


def expert_copies(steps, ny, nz):
    return (steps + 2) * (2 * (ny - 1) + 2 * (nz - 1) + 9 + 7) + ny + nz - 2 + 9


def layer_call(
    plan, lengths, tokens, routes, top, entries, queries, cache, w_gate, w_up, w_down, ny, nz
):
    steps, owned, width = tokens.shape
    block, quarter = NQ * owned, width // NQ
    traces, heads, rows = cache.shape[0], queries.shape[3], cache.shape[2]
    cap = ny * nz * CAP_E
    hidden = w_gate.shape[2]
    copies = expert_copies(steps, ny, nz)
    bf16 = jnp.bfloat16
    any_spec = pl.BlockSpec(memory_space=pl.ANY)
    vmem_spec = pl.BlockSpec(memory_space=pltpu.VMEM)
    smem_spec = pl.BlockSpec(memory_space=pltpu.SMEM)
    contexts = (steps, traces, heads, queries.shape[2] - ROPE)
    return pl.pallas_call(
        partial(layer_kernel, ny, nz, top),
        in_specs=[smem_spec] * 2 + [vmem_spec] * 3 + [any_spec] * 5,
        out_specs=[vmem_spec, vmem_spec, any_spec],
        out_shape=[
            jax.ShapeDtypeStruct(tokens.shape, bf16),
            jax.ShapeDtypeStruct(cache.shape, bf16),
            jax.ShapeDtypeStruct(contexts, bf16),
        ],
        scratch_shapes=[
            pltpu.VMEM((width, hidden), bf16),
            pltpu.VMEM((width, hidden), bf16),
            pltpu.VMEM((hidden, width), bf16),
            pltpu.VMEM(queries.shape, bf16),
            pltpu.VMEM(cache.shape, bf16),
            pltpu.VMEM(contexts, bf16),
            pltpu.VMEM((2 * NX, plan.shape[0] // (4 * NX)) + cache.shape[1:], bf16),
            pltpu.VMEM((ny * nz,) + routes.shape, bf16),
            pltpu.VMEM((ny * nz * block, ny * nz * block), bf16),
            pltpu.VMEM((steps, ny * nz * block, routes.shape[1]), jnp.float32),
            pltpu.VMEM((steps, ny * nz * block, routes.shape[1]), jnp.float32),
            pltpu.VMEM((2, NX * cap, hidden), bf16),
            pltpu.VMEM((steps, ny * nz, block, quarter), bf16),
            pltpu.VMEM((steps, 2 * NX, NQ * cap, quarter), bf16),
            pltpu.VMEM((steps, 2 * NX, NQ * cap, quarter), bf16),
            pltpu.VMEM((steps, NX, NQ * cap, quarter), bf16),
            pltpu.VMEM((steps, 2, NQ * cap // 2, quarter), bf16),
            pltpu.VMEM((steps, 2, NQ * cap, quarter), bf16),
            pltpu.VMEM((NQ * cap, quarter), bf16),
            pltpu.VMEM((steps, ny * nz, block, quarter), bf16),
            pltpu.VMEM((steps, max(ny - 1, 1), nz, block, quarter), bf16),
            pltpu.VMEM((steps, nz, block, quarter), bf16),
            pltpu.VMEM((steps, max(nz - 1, 1), block, quarter), bf16),
            pltpu.SemaphoreType.DMA((6,)),
            pltpu.SemaphoreType.DMA((copies,)),
            pltpu.SemaphoreType.DMA((copies,)),
        ],
        compiler_params=pltpu.CompilerParams(
            collective_id=0, has_side_effects=True, vmem_limit_bytes=60 << 20
        ),
    )(plan, lengths, tokens, routes, entries, queries, cache, w_gate, w_up, w_down)


def narrow(value):
    return lax.reduce_precision(value, exponent_bits=8, mantissa_bits=7)


def body(
    ny, queries, cache, new_entries, lengths, moe_input, expert_ids, route_gains,
    w_gate, w_up, w_down, plan,
):
    group = lax.axis_index("grp")
    nz = lax.axis_size("ep") // ny
    steps, owned, _ = moe_input.shape
    entries = jnp.pad(jnp.swapaxes(new_entries, 0, 1), ((0, 0), (0, 16 - steps), (0, 0)))
    own_ids = lax.dynamic_index_in_dim(expert_ids, group, 1, keepdims=False)
    gains = lax.dynamic_index_in_dim(route_gains, group, 1, keepdims=False)
    top = own_ids.shape[2]
    first = narrow(gains)
    second = narrow(gains - first)
    third = gains - first - second
    routes = jnp.concatenate([own_ids.astype(jnp.float32), first, second, third], axis=2)
    routes = jnp.swapaxes(routes.astype(jnp.bfloat16), 0, 1).reshape(owned, -1)
    routes = jnp.pad(routes, ((0, 0), (0, 128 - routes.shape[1])))
    routes = jnp.broadcast_to(routes[None], (NQ, owned, 128)).reshape(-1, 128)
    out, migrated, contexts = layer_call(
        plan.reshape(-1), lengths, moe_input, routes, top, entries,
        jnp.swapaxes(queries, 2, 3), jnp.swapaxes(cache, 1, 2), w_gate, w_up, w_down, ny, nz,
    )
    return (contexts, jnp.swapaxes(migrated, 1, 2), out)


def solution(mesh):
    return jax.shard_map(
        partial(body, NY),
        mesh=mesh,
        in_specs=(
            P(None, ("grp", "ep"), None, None),
            P(("grp", "ep"), None, None),
            P(None, ("grp", "ep"), None),
            P(("grp", "ep")),
            P(None, ("grp", "ep"), None),
            P(None, None, "ep", None),
            P(None, None, "ep", None),
            P("ep", None, "grp"),
            P("ep", None, "grp"),
            P("ep", "grp", None),
            P(None, "ep", None, None),
        ),
        out_specs=(
            P(None, ("grp", "ep"), None, None),
            P(("grp", "ep"), None, None),
            P(None, ("grp", "ep"), None),
        ),
        check_vma=False,
    )
```

```python
from functools import partial

import jax
import jax.numpy as jnp
from jax import lax
from jax.experimental import pallas as pl
from jax.experimental.pallas import tpu as pltpu
from jax.sharding import PartitionSpec as P

ROPE = 64
SCORE_SCALE = 192.0 ** (-0.5)
NX = 4
NY = 4
NQ = 4
CAP_E = 2
MESH = pl.DeviceIdType.MESH


def layer_kernel(
    ny, nz, top, plan, lengths, tokens, routes, entries, queries_hbm, cache_hbm, wg_hbm, wu_hbm, wd_hbm,
    out, migrated, contexts_hbm, wg, wu, wd, queries, cache, contexts, mb, rt, tri, picks, gain_coarse, gain_fine, hb, tb, xb, pb, r1, ra, rb, yb, db, yr, eb, zr,
    wsem, send_sems, recv_sems,
):
    steps, owned = tokens.shape[0], tokens.shape[1]
    block, quarter = NQ * owned, tokens.shape[2] // NQ
    cap = xb.shape[2] // NQ
    group, expert = lax.axis_index("grp"), lax.axis_index("ep")
    x, c = group // 2, group % 2
    y, z = expert // nz, expert % nz
    right, left, far = (x + 1) % NX, (x + NX - 1) % NX, (x + 2) % NX
    dev_right, dev_left = (right * 2 + c, expert), (left * 2 + c, expert)
    dev_sib = (x * 2 + 1 - c, expert)

    def dev_y(k):
        return (group, ((y + k) % ny) * nz + z)

    def dev_z(k):
        return (group, y * nz + (z + k) % nz)

    peers = [dev_right, dev_left, dev_sib]
    peers += [dev_y(k) for k in range(1, ny)] + [dev_z(k) for k in range(1, nz)]
    barrier = pltpu.get_barrier_semaphore()
    for peer in peers:
        pl.semaphore_signal(barrier, inc=1, device_id=peer, device_id_type=MESH)
    cache_load = pltpu.make_async_copy(cache_hbm, cache, wsem.at[3])
    query_load = pltpu.make_async_copy(queries_hbm, queries, wsem.at[4])
    context_store = pltpu.make_async_copy(contexts, contexts_hbm, wsem.at[5])
    loads = [
        pltpu.make_async_copy(hbm.at[0], vmem, wsem.at[i])
        for i, (hbm, vmem) in enumerate(((wg_hbm, wg), (wu_hbm, wu), (wd_hbm, wd)))
    ]
    for load in [cache_load, query_load] + loads:
        load.start()
    pl.semaphore_wait(barrier, len(peers))

    number = {}
    started = []

    def slot(tag):
        return number.setdefault(tag, len(number))

    def send(tag, src, dst, dev):
        i = slot(tag)
        copy = pltpu.make_async_remote_copy(
            src_ref=src, dst_ref=dst, send_sem=send_sems.at[i], recv_sem=recv_sems.at[i],
            device_id=dev, device_id_type=MESH,
        )
        copy.start()
        started.append(copy)

    def arrived(tag, dst):
        i = slot(tag)
        pltpu.make_async_remote_copy(
            src_ref=dst, dst_ref=dst, send_sem=send_sems.at[i], recv_sem=recv_sems.at[i],
            device_id=dev_right, device_id_type=MESH,
        ).wait_recv()

    def route_z_send():
        rt[expert] = routes[...]
        for k in range(1, nz):
            send(("rz", k), rt.at[expert], rt.at[expert], dev_z(k))

    def route_y_send():
        for k in range(1, nz):
            arrived(("rz", k), rt.at[y * nz + (z + nz - k) % nz])
        part = rt.at[pl.ds(y * nz, nz)]
        for k in range(1, ny):
            send(("ry", k), part, part, dev_y(k))

    def z_send(s, p):
        for k in range(1, nz):
            part = tb.at[s, expert, :, p]
            send(("z", s, p.start, k), part, part, dev_z(k))

    def z_wait(s, p):
        for k in range(1, nz):
            arrived(("z", s, p.start, k), tb.at[s, y * nz + (z + nz - k) % nz, :, p])

    def y_send(s, p):
        part = tb.at[s, pl.ds(y * nz, nz), :, p]
        for k in range(1, ny):
            send(("y", s, p.start, k), part, part, dev_y(k))

    def y_wait(s, p):
        for k in range(1, ny):
            first = (y + ny - k) % ny * nz
            arrived(("y", s, p.start, k), tb.at[s, pl.ds(first, nz), :, p])

    columns = ny * nz * block

    def earlier():
        row = lax.broadcasted_iota(jnp.int32, (columns, columns), 0)
        other = lax.broadcasted_iota(jnp.int32, (columns, columns), 1)
        row_token = row // block * owned + row % owned
        other_token = other // block * owned + other % owned
        counted = ((other // owned) % NQ == 0) & (other_token < row_token)
        tri[...] = jnp.where(counted, 1.0, 0.0).astype(jnp.bfloat16)

    def rank(s):
        if s == 0:
            for k in range(1, ny):
                arrived(("ry", k), rt.at[pl.ds(((y + ny - k) % ny) * nz, nz)])
        route = rt[...].reshape(columns, rt.shape[2]).astype(jnp.float32)
        lane = lax.broadcasted_iota(jnp.int32, route.shape, 1) - 4 * top * s
        hit = (route == expert.astype(jnp.float32)) & (lane >= 0) & (lane < top)
        gains = sum(pltpu.roll(route, rt.shape[2] - k * top, 1) for k in (1, 2, 3))
        gain = jnp.sum(jnp.where(hit, gains, 0.0), axis=1, keepdims=True)
        chosen = jnp.sum(jnp.where(hit, 1.0, 0.0), axis=1, keepdims=True)
        chosen = jnp.broadcast_to(chosen, route.shape)
        before = jnp.dot(tri[...], chosen.astype(jnp.bfloat16), preferred_element_type=jnp.float32)
        rank_of = jnp.where(chosen > 0.5, before, -1.0)[:, 0:1]
        sub = lax.broadcasted_iota(jnp.int32, (columns, NQ * cap), 0)
        slot_at = lax.broadcasted_iota(jnp.int32, (columns, NQ * cap), 1)
        here = (rank_of == (slot_at % cap).astype(jnp.float32)) & (
            (sub // owned) % NQ == slot_at // cap
        )
        picks[s] = jnp.where(here, 1.0, 0.0).T.astype(jnp.bfloat16)
        gain = jnp.where(here, gain, 0.0)
        coarse = gain.astype(jnp.bfloat16)
        gain_coarse[s] = coarse
        gain_fine[s] = (gain - coarse.astype(jnp.float32)).astype(jnp.bfloat16)

    def select(s, p):
        rows = jnp.dot(
            picks[s], tb[s, :, :, p].reshape(columns, p.stop - p.start),
            preferred_element_type=jnp.float32,
        )
        xb[s, c * NX + x, :, p] = rows.astype(jnp.bfloat16)

    half = NQ * cap // 2
    low, high = pl.ds(0, half), pl.ds(half, half)

    def x_own(s, p):
        mine = xb.at[s, c * NX + x, :, p]
        send(("xl", s, p.start), mine, mine, dev_right)
        send(("xr", s, p.start), mine, mine, dev_left)
        send(("so", s, p.start), mine, mine, dev_sib)

    def x_near(s, p):
        from_left, from_right = xb.at[s, c * NX + left], xb.at[s, c * NX + right]
        arrived(("xl", s, p.start), from_left.at[:, p])
        send(("x2l", s, p.start), from_left.at[low, p], from_left.at[low, p], dev_right)
        send(("sl", s, p.start), from_left.at[:, p], from_left.at[:, p], dev_sib)
        arrived(("xr", s, p.start), from_right.at[:, p])
        send(("x2r", s, p.start), from_right.at[high, p], from_right.at[high, p], dev_left)
        send(("sr", s, p.start), from_right.at[:, p], from_right.at[:, p], dev_sib)

    def x_all(s, p):
        across, other = xb.at[s, c * NX + far], (1 - c) * NX
        arrived(("x2l", s, p.start), across.at[low, p])
        send(("s2l", s, p.start), across.at[low, p], across.at[low, p], dev_sib)
        arrived(("x2r", s, p.start), across.at[high, p])
        send(("s2r", s, p.start), across.at[high, p], across.at[high, p], dev_sib)
        arrived(("so", s, p.start), xb.at[s, other + x, :, p])
        arrived(("sl", s, p.start), xb.at[s, other + left, :, p])
        arrived(("sr", s, p.start), xb.at[s, other + right, :, p])
        arrived(("s2l", s, p.start), xb.at[s, other + far, low, p])
        arrived(("s2r", s, p.start), xb.at[s, other + far, high, p])

    def experts(s):
        def part(h, carry):
            gate, up = 0.0, 0.0
            for q in range(NQ):
                rows = xb[s, pl.ds(h * NX, NX), q * cap:(q + 1) * cap, :]
                rows = rows.reshape(NX * cap, quarter)
                cols = slice(q * quarter, (q + 1) * quarter)
                gate += jnp.dot(rows, wg[cols, :], preferred_element_type=jnp.float32)
                up += jnp.dot(rows, wu[cols, :], preferred_element_type=jnp.float32)
            hb[h] = (gate / (1.0 + jnp.exp(-gate)) * up).astype(jnp.bfloat16)
            return carry

        lax.fori_loop(0, 2, part, 0)

    def outputs(s, p):
        def part(h, carry):
            for q in range(NQ):
                cols = slice(q * quarter + p.start, q * quarter + p.stop)
                pb[s, pl.ds(h * NX, NX), q * cap:(q + 1) * cap, p] = (
                    jnp.dot(hb[h], wd[:, cols], preferred_element_type=jnp.float32)
                    .astype(jnp.bfloat16).reshape(NX, cap, p.stop - p.start)
                )
            return carry

        lax.fori_loop(0, 2, part, 0)
        theirs = pb.at[s, pl.ds((1 - c) * NX, NX), :, p]
        send(("r1", s, p.start), theirs, r1.at[s, :, :, p], dev_sib)

    def attend(t):
        filled = lengths[t]
        rows, latent = cache.shape[2], contexts.shape[3]
        at_row = lax.broadcasted_iota(jnp.int32, (16, rows), 1) - filled
        step_of = lax.broadcasted_iota(jnp.int32, (16, rows), 0)
        new = [entries[step].astype(jnp.float32)[t:t + 1] for step in range(steps)]
        new.append(jnp.zeros((16 - steps, entries.shape[2]), jnp.float32))
        new = jnp.concatenate(new, axis=0).astype(jnp.bfloat16)
        place = jnp.where((at_row == step_of) & (step_of < steps), 1.0, 0.0).astype(jnp.bfloat16)
        added = lax.dot_general(
            new, place, (((0,), (0,)), ((), ())), preferred_element_type=jnp.float32
        )
        lane = lax.broadcasted_iota(jnp.int32, (1, rows), 1) - filled
        old = cache[t].astype(jnp.float32)
        keys = jnp.where((lane >= 0) & (lane < steps), added, old)
        cache[t] = keys.astype(jnp.bfloat16)
        keys = keys.T.astype(jnp.bfloat16)
        position = lax.broadcasted_iota(jnp.int32, (rows, 1), 0) - filled
        for step in range(steps):
            scores = jnp.dot(keys, queries[step, t], preferred_element_type=jnp.float32)
            scores = jnp.where(position <= step, scores * SCORE_SCALE, -jnp.inf)
            raised = jnp.exp(scores - jnp.max(scores, axis=0, keepdims=True))
            weights = raised / jnp.sum(raised, axis=0, keepdims=True)
            contexts[step, t] = jnp.dot(
                weights.T.astype(jnp.bfloat16), keys[:, :latent],
                preferred_element_type=jnp.float32,
            ).astype(jnp.bfloat16)

    def m_own():
        mine = c * NX + x
        for k in range(mb.shape[1]):
            mb[mine, k] = cache[plan[0, k, 0, group]]
        send("ml", mb.at[mine], mb.at[mine], dev_right)
        send("mr", mb.at[mine], mb.at[mine], dev_left)
        send("ms", mb.at[mine], mb.at[mine], dev_sib)

    def m_near():
        from_left, from_right = c * NX + left, c * NX + right
        arrived("ml", mb.at[from_left])
        send("m2l", mb.at[from_left, 0], mb.at[from_left, 0], dev_right)
        send("msl", mb.at[from_left], mb.at[from_left], dev_sib)
        arrived("mr", mb.at[from_right])
        send("m2r", mb.at[from_right, 1], mb.at[from_right, 1], dev_left)
        send("msr", mb.at[from_right], mb.at[from_right], dev_sib)

    def m_far():
        across = c * NX + far
        arrived("m2l", mb.at[across, 0])
        send("ms2l", mb.at[across, 0], mb.at[across, 0], dev_sib)
        arrived("m2r", mb.at[across, 1])
        send("ms2r", mb.at[across, 1], mb.at[across, 1], dev_sib)

    def m_take():
        other = (1 - c) * NX
        arrived("ms", mb.at[other + x])
        arrived("msl", mb.at[other + left])
        arrived("msr", mb.at[other + right])
        arrived("ms2l", mb.at[other + far, 0])
        arrived("ms2r", mb.at[other + far, 1])
        entries_sent = mb.shape[1]
        lands, coming = [], []
        for k in range(entries_sent):
            sender = jnp.int32(0)
            for g in range(2 * NX):
                goes = plan[0, k, 1, g]
                sender = jnp.where(goes == group, g % 2 * NX + g // 2, sender)
            coming.append(sender)
            lands.append(plan[0, k, 0, group])

        def place(t, carry):
            value = cache[t].astype(jnp.float32)
            for k in range(entries_sent):
                here = jnp.broadcast_to(lands[k] - t, value.shape) == 0
                value = jnp.where(here, mb[coming[k], k].astype(jnp.float32), value)
            migrated[t] = value.astype(jnp.bfloat16)
            return carry

        lax.fori_loop(0, cache.shape[0], place, 0)

    piece = 32

    def add_into(dst, other, first, rows, p, shift=0):
        def part(i, carry):
            at = pl.ds(pl.multiple_of(first + i * piece, piece), piece)
            inner = pl.ds(pl.multiple_of(first - shift + i * piece, piece), piece)
            total = dst[at, p].astype(jnp.float32) + other[inner, p].astype(jnp.float32)
            dst[at, p] = total.astype(jnp.bfloat16)
            return carry

        lax.fori_loop(0, rows // piece, part, 0)

    def r1_add(s, p):
        arrived(("r1", s, p.start), r1.at[s, :, :, p])
        to_far, to_right, to_left = c * NX + far, c * NX + right, c * NX + left
        add_into(pb.at[s, to_far], r1.at[s, far], 0, 2 * half, p)
        send(("ral", s, p.start), pb.at[s, to_far, low, p], ra.at[s, 0, :, p], dev_right)
        send(("rar", s, p.start), pb.at[s, to_far, high, p], ra.at[s, 1, :, p], dev_left)
        add_into(pb.at[s, to_right], r1.at[s, right], 0, 2 * half, p)
        send(("rbl", s, p.start, 1), pb.at[s, to_right, high, p], rb.at[s, 0, high, p], dev_right)
        add_into(pb.at[s, to_left], r1.at[s, left], 0, 2 * half, p)
        send(("rbr", s, p.start, 0), pb.at[s, to_left, low, p], rb.at[s, 1, low, p], dev_left)

    def ra_add(s, p):
        to_right, to_left = c * NX + right, c * NX + left
        arrived(("ral", s, p.start), ra.at[s, 0, :, p])
        add_into(pb.at[s, to_right], ra.at[s, 0], 0, half, p)
        send(("rbl", s, p.start, 0), pb.at[s, to_right, low, p], rb.at[s, 0, low, p], dev_right)
        arrived(("rar", s, p.start), ra.at[s, 1, :, p])
        add_into(pb.at[s, to_left], ra.at[s, 1], half, half, p, half)
        send(("rbr", s, p.start, 1), pb.at[s, to_left, high, p], rb.at[s, 1, high, p], dev_left)

    def combine(s, p):
        arrived(("rbl", s, p.start, 1), rb.at[s, 0, high, p])
        arrived(("rbr", s, p.start, 0), rb.at[s, 1, low, p])
        arrived(("rbl", s, p.start, 0), rb.at[s, 0, low, p])
        arrived(("rbr", s, p.start, 1), rb.at[s, 1, high, p])

        def final(i, carry):
            at = pl.ds(pl.multiple_of(i * piece, piece), piece)
            total = pb[s, c * NX + x, at, p].astype(jnp.float32)
            total += r1[s, x, at, p].astype(jnp.float32)
            total += rb[s, 0, at, p].astype(jnp.float32) + rb[s, 1, at, p].astype(jnp.float32)
            yb[at, p] = total.astype(jnp.bfloat16)
            return carry

        lax.fori_loop(0, NQ * cap // piece, final, 0)
        rows = nz * block

        def part(i, carry):
            first = pl.multiple_of(i * rows, rows)
            at = pl.ds(first, rows)
            total = jnp.dot(gain_coarse[s, at], yb[:, p], preferred_element_type=jnp.float32)
            total += jnp.dot(gain_fine[s, at], yb[:, p], preferred_element_type=jnp.float32)
            db[s, pl.ds(i * nz, nz), :, p] = (
                total.astype(jnp.bfloat16).reshape(nz, block, p.stop - p.start)
            )
            return carry

        lax.fori_loop(0, ny, part, 0)
        for k in range(1, ny):
            theirs = db.at[s, pl.ds((y + k) % ny * nz, nz), :, p]
            send(("yr", s, p.start, k), theirs, yr.at[s, k - 1, :, :, p], dev_y(k))

    def y_sum(s, p):
        for k in range(1, ny):
            arrived(("yr", s, p.start, k), yr.at[s, k - 1, :, :, p])

        def part(i, carry):
            total = db[s, y * nz + i, :, p].astype(jnp.float32)
            for k in range(1, ny):
                total += yr[s, k - 1, i, :, p].astype(jnp.float32)
            eb[s, i, :, p] = total.astype(jnp.bfloat16)
            return carry

        lax.fori_loop(0, nz, part, 0)
        for k in range(1, nz):
            theirs = eb.at[s, (z + k) % nz, :, p]
            send(("zr", s, p.start, k), theirs, zr.at[s, k - 1, :, p], dev_z(k))

    def z_sum(s, p):
        total = eb[s, z, :, p].astype(jnp.float32)
        for k in range(1, nz):
            arrived(("zr", s, p.start, k), zr.at[s, k - 1, :, p])
            total += zr[s, k - 1, :, p].astype(jnp.float32)
        for q in range(NQ):
            cols = slice(q * quarter + p.start, q * quarter + p.stop)
            out[s, :, cols] = total[q * owned:(q + 1) * owned].astype(jnp.bfloat16)

    whole = slice(0, quarter)
    tiles = quarter // 128
    a = max(tiles // 7, 1) * 128
    b = a + max(2 * tiles // 7, 1) * 128
    enter = [slice(0, a), slice(a, b), slice(b, quarter)]
    leave = [slice(0, quarter - b), slice(quarter - b, quarter - a), slice(quarter - a, quarter)]

    route_z_send()
    for s in range(steps):
        row = tokens[s].astype(jnp.float32)
        row = [row[:, q * quarter:(q + 1) * quarter] for q in range(NQ)]
        tb[s, expert] = jnp.concatenate(row, axis=0).astype(jnp.bfloat16)
    for p in enter:
        z_send(0, p)
    earlier()
    route_y_send()
    for p in enter:
        z_wait(0, p), y_send(0, p)
    z_send(1, whole)
    rank(0)
    for p in enter:
        y_wait(0, p)
        select(0, p), x_own(0, p)
    z_wait(1, whole), y_send(1, whole), z_send(2, whole)
    rank(1), rank(2)
    cache_load.wait(), query_load.wait()
    attend(0)
    for p in enter:
        x_near(0, p)
    y_wait(1, whole), select(1, whole), x_own(1, whole)
    z_wait(2, whole), y_send(2, whole)
    for p in enter:
        x_all(0, p)
    for load in loads:
        load.wait()
    experts(0), outputs(0, whole)
    attend(1)
    x_near(1, whole)
    y_wait(2, whole), select(2, whole), x_own(2, whole)
    r1_add(0, whole)
    x_all(1, whole)
    experts(1), outputs(1, whole)
    ra_add(0, whole)
    attend(2)
    x_near(2, whole)
    r1_add(1, whole)
    attend(3)
    context_store.start()
    x_all(2, whole)
    experts(2)
    for p in leave:
        outputs(2, p)
    combine(0, whole)
    ra_add(1, whole)
    for p in leave:
        r1_add(2, p)
    y_sum(0, whole)
    combine(1, whole)
    for p in leave:
        ra_add(2, p)
    m_own()
    z_sum(0, whole)
    y_sum(1, whole)
    for p in leave:
        combine(2, p)
    z_sum(1, whole)
    m_near()
    for p in leave:
        y_sum(2, p)
    m_far()
    for p in leave:
        z_sum(2, p)
    m_take()
    context_store.wait()
    for copy in started:
        copy.wait_send()


def expert_copies(steps, ny, nz):
    return (steps + 2) * (2 * (ny - 1) + 2 * (nz - 1) + 9 + 7) + ny + nz - 2 + 9


def layer_call(
    plan, lengths, tokens, routes, top, entries, queries, cache, w_gate, w_up, w_down, ny, nz
):
    steps, owned, width = tokens.shape
    block, quarter = NQ * owned, width // NQ
    traces, heads, rows = cache.shape[0], queries.shape[3], cache.shape[2]
    cap = ny * nz * CAP_E
    hidden = w_gate.shape[2]
    copies = expert_copies(steps, ny, nz)
    bf16 = jnp.bfloat16
    any_spec = pl.BlockSpec(memory_space=pl.ANY)
    vmem_spec = pl.BlockSpec(memory_space=pltpu.VMEM)
    smem_spec = pl.BlockSpec(memory_space=pltpu.SMEM)
    contexts = (steps, traces, heads, queries.shape[2] - ROPE)
    return pl.pallas_call(
        partial(layer_kernel, ny, nz, top),
        in_specs=[smem_spec] * 2 + [vmem_spec] * 3 + [any_spec] * 5,
        out_specs=[vmem_spec, vmem_spec, any_spec],
        out_shape=[
            jax.ShapeDtypeStruct(tokens.shape, bf16),
            jax.ShapeDtypeStruct(cache.shape, bf16),
            jax.ShapeDtypeStruct(contexts, bf16),
        ],
        scratch_shapes=[
            pltpu.VMEM((width, hidden), bf16),
            pltpu.VMEM((width, hidden), bf16),
            pltpu.VMEM((hidden, width), bf16),
            pltpu.VMEM(queries.shape, bf16),
            pltpu.VMEM(cache.shape, bf16),
            pltpu.VMEM(contexts, bf16),
            pltpu.VMEM((2 * NX, plan.shape[1]) + cache.shape[1:], bf16),
            pltpu.VMEM((ny * nz,) + routes.shape, bf16),
            pltpu.VMEM((ny * nz * block, ny * nz * block), bf16),
            pltpu.VMEM((steps, NQ * cap, ny * nz * block), bf16),
            pltpu.VMEM((steps, ny * nz * block, NQ * cap), bf16),
            pltpu.VMEM((steps, ny * nz * block, NQ * cap), bf16),
            pltpu.VMEM((2, NX * cap, hidden), bf16),
            pltpu.VMEM((steps, ny * nz, block, quarter), bf16),
            pltpu.VMEM((steps, 2 * NX, NQ * cap, quarter), bf16),
            pltpu.VMEM((steps, 2 * NX, NQ * cap, quarter), bf16),
            pltpu.VMEM((steps, NX, NQ * cap, quarter), bf16),
            pltpu.VMEM((steps, 2, NQ * cap // 2, quarter), bf16),
            pltpu.VMEM((steps, 2, NQ * cap, quarter), bf16),
            pltpu.VMEM((NQ * cap, quarter), bf16),
            pltpu.VMEM((steps, ny * nz, block, quarter), bf16),
            pltpu.VMEM((steps, max(ny - 1, 1), nz, block, quarter), bf16),
            pltpu.VMEM((steps, nz, block, quarter), bf16),
            pltpu.VMEM((steps, max(nz - 1, 1), block, quarter), bf16),
            pltpu.SemaphoreType.DMA((6,)),
            pltpu.SemaphoreType.DMA((copies,)),
            pltpu.SemaphoreType.DMA((copies,)),
        ],
        compiler_params=pltpu.CompilerParams(
            collective_id=0, has_side_effects=True, vmem_limit_bytes=60 << 20
        ),
    )(plan, lengths, tokens, routes, entries, queries, cache, w_gate, w_up, w_down)


def narrow(value):
    return lax.reduce_precision(value, exponent_bits=8, mantissa_bits=7)


def body(
    ny, queries, cache, new_entries, lengths, moe_input, expert_ids, route_gains,
    w_gate, w_up, w_down, plan,
):
    group = lax.axis_index("grp")
    nz = lax.axis_size("ep") // ny
    steps, owned, _ = moe_input.shape
    own_ids = lax.dynamic_index_in_dim(expert_ids, group, 1, keepdims=False)
    gains = lax.dynamic_index_in_dim(route_gains, group, 1, keepdims=False)
    top = own_ids.shape[2]
    first = narrow(gains)
    second = narrow(gains - first)
    third = gains - first - second
    routes = jnp.concatenate([own_ids.astype(jnp.float32), first, second, third], axis=2)
    routes = jnp.swapaxes(routes.astype(jnp.bfloat16), 0, 1).reshape(owned, -1)
    routes = jnp.pad(routes, ((0, 0), (0, 128 - routes.shape[1])))
    routes = jnp.broadcast_to(routes[None], (NQ, owned, 128)).reshape(-1, 128)
    out, migrated, contexts = layer_call(
        jnp.transpose(plan, (1, 2, 3, 0)), lengths, moe_input, routes, top, new_entries,
        jnp.swapaxes(queries, 2, 3), jnp.swapaxes(cache, 1, 2), w_gate, w_up, w_down, ny, nz,
    )
    return (contexts, jnp.swapaxes(migrated, 1, 2), out)


def solution(mesh):
    return jax.shard_map(
        partial(body, NY),
        mesh=mesh,
        in_specs=(
            P(None, ("grp", "ep"), None, None),
            P(("grp", "ep"), None, None),
            P(None, ("grp", "ep"), None),
            P(("grp", "ep")),
            P(None, ("grp", "ep"), None),
            P(None, None, "ep", None),
            P(None, None, "ep", None),
            P("ep", None, "grp"),
            P("ep", None, "grp"),
            P("ep", "grp", None),
            P(None, "ep", None, None),
        ),
        out_specs=(
            P(None, ("grp", "ep"), None, None),
            P(("grp", "ep"), None, None),
            P(None, ("grp", "ep"), None),
        ),
        check_vma=False,
    )
```

```python
from functools import partial

import jax
import jax.numpy as jnp
from jax import lax
from jax.experimental import pallas as pl
from jax.experimental.pallas import tpu as pltpu
from jax.sharding import PartitionSpec as P

ROPE = 64
SCORE_SCALE = 192.0 ** (-0.5)
NX = 4
NY = 4
NQ = 4
CAP_E = 2
MESH = pl.DeviceIdType.MESH


def layer_kernel(
    ny, nz, top, plan, lengths, tokens, routes, entries, queries_hbm, cache_hbm, wg_hbm, wu_hbm, wd_hbm,
    out, migrated, contexts_hbm, wg, wu, wd, queries, cache, contexts, mb, rt, tri, picks, gain_coarse, gain_fine, hb, tb, xb, pb, r1, ra, rb, yb, db, yr, eb, zr,
    wsem, send_sems, recv_sems,
):
    steps, owned = tokens.shape[0], tokens.shape[1]
    block, quarter = NQ * owned, tokens.shape[2] // NQ
    cap = xb.shape[2] // NQ
    group, expert = lax.axis_index("grp"), lax.axis_index("ep")
    x, c = group // 2, group % 2
    y, z = expert // nz, expert % nz
    right, left, far = (x + 1) % NX, (x + NX - 1) % NX, (x + 2) % NX
    dev_right, dev_left = (right * 2 + c, expert), (left * 2 + c, expert)
    dev_sib = (x * 2 + 1 - c, expert)

    def dev_y(k):
        return (group, ((y + k) % ny) * nz + z)

    def dev_z(k):
        return (group, y * nz + (z + k) % nz)

    peers = [dev_right, dev_left, dev_sib]
    peers += [dev_y(k) for k in range(1, ny)] + [dev_z(k) for k in range(1, nz)]
    barrier = pltpu.get_barrier_semaphore()
    for peer in peers:
        pl.semaphore_signal(barrier, inc=1, device_id=peer, device_id_type=MESH)
    cache_load = pltpu.make_async_copy(cache_hbm, cache, wsem.at[3])
    query_load = pltpu.make_async_copy(queries_hbm, queries, wsem.at[4])
    context_store = pltpu.make_async_copy(contexts, contexts_hbm, wsem.at[5])
    loads = [
        pltpu.make_async_copy(hbm.at[0], vmem, wsem.at[i])
        for i, (hbm, vmem) in enumerate(((wg_hbm, wg), (wu_hbm, wu), (wd_hbm, wd)))
    ]
    for load in [cache_load, query_load] + loads:
        load.start()
    pl.semaphore_wait(barrier, len(peers))

    number = {}
    started = []

    def slot(tag):
        return number.setdefault(tag, len(number))

    def send(tag, src, dst, dev):
        i = slot(tag)
        copy = pltpu.make_async_remote_copy(
            src_ref=src, dst_ref=dst, send_sem=send_sems.at[i], recv_sem=recv_sems.at[i],
            device_id=dev, device_id_type=MESH,
        )
        copy.start()
        started.append(copy)

    def arrived(tag, dst):
        i = slot(tag)
        pltpu.make_async_remote_copy(
            src_ref=dst, dst_ref=dst, send_sem=send_sems.at[i], recv_sem=recv_sems.at[i],
            device_id=dev_right, device_id_type=MESH,
        ).wait_recv()

    def route_z_send():
        rt[expert] = routes[...]
        for k in range(1, nz):
            send(("rz", k), rt.at[expert], rt.at[expert], dev_z(k))

    def route_y_send():
        for k in range(1, nz):
            arrived(("rz", k), rt.at[y * nz + (z + nz - k) % nz])
        part = rt.at[pl.ds(y * nz, nz)]
        for k in range(1, ny):
            send(("ry", k), part, part, dev_y(k))

    def z_send(s, p):
        for k in range(1, nz):
            part = tb.at[s, expert, :, p]
            send(("z", s, p.start, k), part, part, dev_z(k))

    def z_wait(s, p):
        for k in range(1, nz):
            arrived(("z", s, p.start, k), tb.at[s, y * nz + (z + nz - k) % nz, :, p])

    def y_send(s, p):
        part = tb.at[s, pl.ds(y * nz, nz), :, p]
        for k in range(1, ny):
            send(("y", s, p.start, k), part, part, dev_y(k))

    def y_wait(s, p):
        for k in range(1, ny):
            first = (y + ny - k) % ny * nz
            arrived(("y", s, p.start, k), tb.at[s, pl.ds(first, nz), :, p])

    columns = ny * nz * block

    def earlier():
        row = lax.broadcasted_iota(jnp.int32, (columns, columns), 0)
        other = lax.broadcasted_iota(jnp.int32, (columns, columns), 1)
        row_token = row // block * owned + row % owned
        other_token = other // block * owned + other % owned
        counted = ((other // owned) % NQ == 0) & (other_token < row_token)
        tri[...] = jnp.where(counted, 1.0, 0.0).astype(jnp.bfloat16)

    def rank(s):
        if s == 0:
            for k in range(1, ny):
                arrived(("ry", k), rt.at[pl.ds(((y + ny - k) % ny) * nz, nz)])
        route = rt[...].reshape(columns, rt.shape[2]).astype(jnp.float32)
        lane = lax.broadcasted_iota(jnp.int32, route.shape, 1) - 4 * top * s
        hit = (route == expert.astype(jnp.float32)) & (lane >= 0) & (lane < top)
        gains = sum(pltpu.roll(route, rt.shape[2] - k * top, 1) for k in (1, 2, 3))
        gain = jnp.sum(jnp.where(hit, gains, 0.0), axis=1, keepdims=True)
        chosen = jnp.sum(jnp.where(hit, 1.0, 0.0), axis=1, keepdims=True)
        chosen = jnp.broadcast_to(chosen, route.shape)
        before = jnp.dot(tri[...], chosen.astype(jnp.bfloat16), preferred_element_type=jnp.float32)
        rank_of = jnp.where(chosen > 0.5, before, -1.0)[:, 0:1]
        sub = lax.broadcasted_iota(jnp.int32, (columns, NQ * cap), 0)
        slot_at = lax.broadcasted_iota(jnp.int32, (columns, NQ * cap), 1)
        here = (rank_of == (slot_at % cap).astype(jnp.float32)) & (
            (sub // owned) % NQ == slot_at // cap
        )
        picks[s] = jnp.where(here, 1.0, 0.0).T.astype(jnp.bfloat16)
        gain = jnp.where(here, gain, 0.0)
        coarse = gain.astype(jnp.bfloat16)
        gain_coarse[s] = coarse
        gain_fine[s] = (gain - coarse.astype(jnp.float32)).astype(jnp.bfloat16)

    def select(s, p):
        rows = jnp.dot(
            picks[s], tb[s, :, :, p].reshape(columns, p.stop - p.start),
            preferred_element_type=jnp.float32,
        )
        xb[s, c * NX + x, :, p] = rows.astype(jnp.bfloat16)

    half = NQ * cap // 2
    low, high = pl.ds(0, half), pl.ds(half, half)

    def x_own(s, p):
        mine = xb.at[s, c * NX + x, :, p]
        send(("xl", s, p.start), mine, mine, dev_right)
        send(("xr", s, p.start), mine, mine, dev_left)
        send(("so", s, p.start), mine, mine, dev_sib)

    def x_near(s, p):
        from_left, from_right = xb.at[s, c * NX + left], xb.at[s, c * NX + right]
        arrived(("xl", s, p.start), from_left.at[:, p])
        send(("x2l", s, p.start), from_left.at[low, p], from_left.at[low, p], dev_right)
        send(("sl", s, p.start), from_left.at[:, p], from_left.at[:, p], dev_sib)
        arrived(("xr", s, p.start), from_right.at[:, p])
        send(("x2r", s, p.start), from_right.at[high, p], from_right.at[high, p], dev_left)
        send(("sr", s, p.start), from_right.at[:, p], from_right.at[:, p], dev_sib)

    def x_all(s, p):
        across, other = xb.at[s, c * NX + far], (1 - c) * NX
        arrived(("x2l", s, p.start), across.at[low, p])
        send(("s2l", s, p.start), across.at[low, p], across.at[low, p], dev_sib)
        arrived(("x2r", s, p.start), across.at[high, p])
        send(("s2r", s, p.start), across.at[high, p], across.at[high, p], dev_sib)
        arrived(("so", s, p.start), xb.at[s, other + x, :, p])
        arrived(("sl", s, p.start), xb.at[s, other + left, :, p])
        arrived(("sr", s, p.start), xb.at[s, other + right, :, p])
        arrived(("s2l", s, p.start), xb.at[s, other + far, low, p])
        arrived(("s2r", s, p.start), xb.at[s, other + far, high, p])

    def experts(s):
        def part(h, carry):
            gate, up = 0.0, 0.0
            for q in range(NQ):
                rows = xb[s, pl.ds(h * NX, NX), q * cap:(q + 1) * cap, :]
                rows = rows.reshape(NX * cap, quarter)
                cols = slice(q * quarter, (q + 1) * quarter)
                gate += jnp.dot(rows, wg[cols, :], preferred_element_type=jnp.float32)
                up += jnp.dot(rows, wu[cols, :], preferred_element_type=jnp.float32)
            hb[h] = (gate / (1.0 + jnp.exp(-gate)) * up).astype(jnp.bfloat16)
            return carry

        lax.fori_loop(0, 2, part, 0)

    def outputs(s, p):
        def part(h, carry):
            for q in range(NQ):
                cols = slice(q * quarter + p.start, q * quarter + p.stop)
                pb[s, pl.ds(h * NX, NX), q * cap:(q + 1) * cap, p] = (
                    jnp.dot(hb[h], wd[:, cols], preferred_element_type=jnp.float32)
                    .astype(jnp.bfloat16).reshape(NX, cap, p.stop - p.start)
                )
            return carry

        lax.fori_loop(0, 2, part, 0)
        theirs = pb.at[s, pl.ds((1 - c) * NX, NX), :, p]
        send(("r1", s, p.start), theirs, r1.at[s, :, :, p], dev_sib)

    def attend(t):
        filled = lengths[t]
        rows, latent = cache.shape[2], contexts.shape[3]
        at_row = lax.broadcasted_iota(jnp.int32, (16, rows), 1) - filled
        step_of = lax.broadcasted_iota(jnp.int32, (16, rows), 0)
        new = [entries[step].astype(jnp.float32)[t:t + 1] for step in range(steps)]
        new.append(jnp.zeros((16 - steps, entries.shape[2]), jnp.float32))
        new = jnp.concatenate(new, axis=0).astype(jnp.bfloat16)
        place = jnp.where((at_row == step_of) & (step_of < steps), 1.0, 0.0).astype(jnp.bfloat16)
        added = lax.dot_general(
            new, place, (((0,), (0,)), ((), ())), preferred_element_type=jnp.float32
        )
        lane = lax.broadcasted_iota(jnp.int32, (1, rows), 1) - filled
        old = cache[t].astype(jnp.float32)
        keys = jnp.where((lane >= 0) & (lane < steps), added, old)
        cache[t] = keys.astype(jnp.bfloat16)
        keys = keys.T.astype(jnp.bfloat16)
        position = lax.broadcasted_iota(jnp.int32, (rows, 1), 0) - filled
        for step in range(steps):
            scores = jnp.dot(keys, queries[step, t], preferred_element_type=jnp.float32)
            scores = jnp.where(position <= step, scores * SCORE_SCALE, -jnp.inf)
            raised = jnp.exp(scores - jnp.max(scores, axis=0, keepdims=True))
            weights = raised / jnp.sum(raised, axis=0, keepdims=True)
            contexts[step, t] = jnp.dot(
                weights.T.astype(jnp.bfloat16), keys[:, :latent],
                preferred_element_type=jnp.float32,
            ).astype(jnp.bfloat16)

    def m_own():
        mine = c * NX + x
        for k in range(mb.shape[1]):
            mb[mine, k] = cache[plan[0, k, 0, group]]
        send("ml", mb.at[mine], mb.at[mine], dev_right)
        send("mr", mb.at[mine], mb.at[mine], dev_left)
        send("ms", mb.at[mine], mb.at[mine], dev_sib)

    def m_near():
        from_left, from_right = c * NX + left, c * NX + right
        arrived("ml", mb.at[from_left])
        send("m2l", mb.at[from_left, 0], mb.at[from_left, 0], dev_right)
        send("msl", mb.at[from_left], mb.at[from_left], dev_sib)
        arrived("mr", mb.at[from_right])
        send("m2r", mb.at[from_right, 1], mb.at[from_right, 1], dev_left)
        send("msr", mb.at[from_right], mb.at[from_right], dev_sib)

    def m_far():
        across = c * NX + far
        arrived("m2l", mb.at[across, 0])
        send("ms2l", mb.at[across, 0], mb.at[across, 0], dev_sib)
        arrived("m2r", mb.at[across, 1])
        send("ms2r", mb.at[across, 1], mb.at[across, 1], dev_sib)

    def m_take():
        other = (1 - c) * NX
        arrived("ms", mb.at[other + x])
        arrived("msl", mb.at[other + left])
        arrived("msr", mb.at[other + right])
        arrived("ms2l", mb.at[other + far, 0])
        arrived("ms2r", mb.at[other + far, 1])
        entries_sent = mb.shape[1]
        lands, coming = [], []
        for k in range(entries_sent):
            sender = jnp.int32(0)
            for g in range(2 * NX):
                goes = plan[0, k, 1, g]
                sender = jnp.where(goes == group, g % 2 * NX + g // 2, sender)
            coming.append(sender)
            lands.append(plan[0, k, 0, group])

        def place(t, carry):
            value = cache[t].astype(jnp.float32)
            for k in range(entries_sent):
                here = jnp.broadcast_to(lands[k] - t, value.shape) == 0
                value = jnp.where(here, mb[coming[k], k].astype(jnp.float32), value)
            migrated[t] = value.astype(jnp.bfloat16)
            return carry

        lax.fori_loop(0, cache.shape[0], place, 0)

    piece = 32

    def add_into(dst, other, first, rows, p, shift=0):
        def part(i, carry):
            at = pl.ds(pl.multiple_of(first + i * piece, piece), piece)
            inner = pl.ds(pl.multiple_of(first - shift + i * piece, piece), piece)
            total = dst[at, p].astype(jnp.float32) + other[inner, p].astype(jnp.float32)
            dst[at, p] = total.astype(jnp.bfloat16)
            return carry

        lax.fori_loop(0, rows // piece, part, 0)

    def r1_add(s, p):
        arrived(("r1", s, p.start), r1.at[s, :, :, p])
        to_far, to_right, to_left = c * NX + far, c * NX + right, c * NX + left
        add_into(pb.at[s, to_far], r1.at[s, far], 0, 2 * half, p)
        send(("ral", s, p.start), pb.at[s, to_far, low, p], ra.at[s, 0, :, p], dev_right)
        send(("rar", s, p.start), pb.at[s, to_far, high, p], ra.at[s, 1, :, p], dev_left)
        add_into(pb.at[s, to_right], r1.at[s, right], 0, 2 * half, p)
        send(("rbl", s, p.start, 1), pb.at[s, to_right, high, p], rb.at[s, 0, high, p], dev_right)
        add_into(pb.at[s, to_left], r1.at[s, left], 0, 2 * half, p)
        send(("rbr", s, p.start, 0), pb.at[s, to_left, low, p], rb.at[s, 1, low, p], dev_left)

    def ra_add(s, p):
        to_right, to_left = c * NX + right, c * NX + left
        arrived(("ral", s, p.start), ra.at[s, 0, :, p])
        add_into(pb.at[s, to_right], ra.at[s, 0], 0, half, p)
        send(("rbl", s, p.start, 0), pb.at[s, to_right, low, p], rb.at[s, 0, low, p], dev_right)
        arrived(("rar", s, p.start), ra.at[s, 1, :, p])
        add_into(pb.at[s, to_left], ra.at[s, 1], half, half, p, half)
        send(("rbr", s, p.start, 1), pb.at[s, to_left, high, p], rb.at[s, 1, high, p], dev_left)

    def combine(s, p):
        arrived(("rbl", s, p.start, 1), rb.at[s, 0, high, p])
        arrived(("rbr", s, p.start, 0), rb.at[s, 1, low, p])
        arrived(("rbl", s, p.start, 0), rb.at[s, 0, low, p])
        arrived(("rbr", s, p.start, 1), rb.at[s, 1, high, p])

        def final(i, carry):
            at = pl.ds(pl.multiple_of(i * piece, piece), piece)
            total = pb[s, c * NX + x, at, p].astype(jnp.float32)
            total += r1[s, x, at, p].astype(jnp.float32)
            total += rb[s, 0, at, p].astype(jnp.float32) + rb[s, 1, at, p].astype(jnp.float32)
            yb[at, p] = total.astype(jnp.bfloat16)
            return carry

        lax.fori_loop(0, NQ * cap // piece, final, 0)
        rows = nz * block

        def part(i, carry):
            first = pl.multiple_of(i * rows, rows)
            at = pl.ds(first, rows)
            total = jnp.dot(gain_coarse[s, at], yb[:, p], preferred_element_type=jnp.float32)
            total += jnp.dot(gain_fine[s, at], yb[:, p], preferred_element_type=jnp.float32)
            db[s, pl.ds(i * nz, nz), :, p] = (
                total.astype(jnp.bfloat16).reshape(nz, block, p.stop - p.start)
            )
            return carry

        lax.fori_loop(0, ny, part, 0)
        for k in range(1, ny):
            theirs = db.at[s, pl.ds((y + k) % ny * nz, nz), :, p]
            send(("yr", s, p.start, k), theirs, yr.at[s, k - 1, :, :, p], dev_y(k))

    def y_sum(s, p):
        for k in range(1, ny):
            arrived(("yr", s, p.start, k), yr.at[s, k - 1, :, :, p])

        def part(i, carry):
            total = db[s, y * nz + i, :, p].astype(jnp.float32)
            for k in range(1, ny):
                total += yr[s, k - 1, i, :, p].astype(jnp.float32)
            eb[s, i, :, p] = total.astype(jnp.bfloat16)
            return carry

        lax.fori_loop(0, nz, part, 0)
        for k in range(1, nz):
            theirs = eb.at[s, (z + k) % nz, :, p]
            send(("zr", s, p.start, k), theirs, zr.at[s, k - 1, :, p], dev_z(k))

    def z_sum(s, p):
        total = eb[s, z, :, p].astype(jnp.float32)
        for k in range(1, nz):
            arrived(("zr", s, p.start, k), zr.at[s, k - 1, :, p])
            total += zr[s, k - 1, :, p].astype(jnp.float32)
        for q in range(NQ):
            cols = slice(q * quarter + p.start, q * quarter + p.stop)
            out[s, :, cols] = total[q * owned:(q + 1) * owned].astype(jnp.bfloat16)

    whole = slice(0, quarter)
    tiles = quarter // 128
    a = max(tiles // 7, 1) * 128
    b = a + max(2 * tiles // 7, 1) * 128
    enter = [slice(0, a), slice(a, b), slice(b, quarter)]
    two = [slice(0, (tiles + 1) // 2 * 128), slice((tiles + 1) // 2 * 128, quarter)]
    leave = [slice(0, quarter - b), slice(quarter - b, quarter - a), slice(quarter - a, quarter)]

    route_z_send()
    for s in range(steps):
        row = tokens[s].astype(jnp.float32)
        row = [row[:, q * quarter:(q + 1) * quarter] for q in range(NQ)]
        tb[s, expert] = jnp.concatenate(row, axis=0).astype(jnp.bfloat16)
    for p in enter:
        z_send(0, p)
    earlier()
    route_y_send()
    for p in enter:
        z_wait(0, p), y_send(0, p)
    z_send(1, whole)
    rank(0)
    for p in enter:
        y_wait(0, p)
        select(0, p), x_own(0, p)
    z_wait(1, whole), y_send(1, whole), z_send(2, whole)
    rank(1), rank(2)
    cache_load.wait(), query_load.wait()
    attend(0)
    for p in enter:
        x_near(0, p)
    y_wait(1, whole), select(1, whole), x_own(1, whole)
    z_wait(2, whole), y_send(2, whole)
    for p in enter:
        x_all(0, p)
    for load in loads:
        load.wait()
    experts(0)
    for p in two:
        outputs(0, p)
    attend(1)
    x_near(1, whole)
    y_wait(2, whole), select(2, whole), x_own(2, whole)
    for p in two:
        r1_add(0, p)
    x_all(1, whole)
    experts(1)
    for p in two:
        outputs(1, p)
    for p in two:
        ra_add(0, p)
    attend(2)
    x_near(2, whole)
    for p in two:
        r1_add(1, p)
    attend(3)
    context_store.start()
    x_all(2, whole)
    experts(2)
    for p in leave:
        outputs(2, p)
    for p in two:
        combine(0, p)
    for p in two:
        ra_add(1, p)
    for p in leave:
        r1_add(2, p)
    for p in two:
        y_sum(0, p)
    for p in two:
        combine(1, p)
    for p in leave:
        ra_add(2, p)
    m_own()
    for p in two:
        z_sum(0, p)
    for p in two:
        y_sum(1, p)
    for p in leave:
        combine(2, p)
    for p in two:
        z_sum(1, p)
    m_near()
    for p in leave:
        y_sum(2, p)
    m_far()
    for p in leave:
        z_sum(2, p)
    m_take()
    context_store.wait()
    for copy in started:
        copy.wait_send()


def expert_copies(steps, ny, nz):
    return (steps + 4) * (2 * (ny - 1) + 2 * (nz - 1) + 9 + 7) + ny + nz - 2 + 9


def layer_call(
    plan, lengths, tokens, routes, top, entries, queries, cache, w_gate, w_up, w_down, ny, nz
):
    steps, owned, width = tokens.shape
    block, quarter = NQ * owned, width // NQ
    traces, heads, rows = cache.shape[0], queries.shape[3], cache.shape[2]
    cap = ny * nz * CAP_E
    hidden = w_gate.shape[2]
    copies = expert_copies(steps, ny, nz)
    bf16 = jnp.bfloat16
    any_spec = pl.BlockSpec(memory_space=pl.ANY)
    vmem_spec = pl.BlockSpec(memory_space=pltpu.VMEM)
    smem_spec = pl.BlockSpec(memory_space=pltpu.SMEM)
    contexts = (steps, traces, heads, queries.shape[2] - ROPE)
    return pl.pallas_call(
        partial(layer_kernel, ny, nz, top),
        in_specs=[smem_spec] * 2 + [vmem_spec] * 3 + [any_spec] * 5,
        out_specs=[vmem_spec, vmem_spec, any_spec],
        out_shape=[
            jax.ShapeDtypeStruct(tokens.shape, bf16),
            jax.ShapeDtypeStruct(cache.shape, bf16),
            jax.ShapeDtypeStruct(contexts, bf16),
        ],
        scratch_shapes=[
            pltpu.VMEM((width, hidden), bf16),
            pltpu.VMEM((width, hidden), bf16),
            pltpu.VMEM((hidden, width), bf16),
            pltpu.VMEM(queries.shape, bf16),
            pltpu.VMEM(cache.shape, bf16),
            pltpu.VMEM(contexts, bf16),
            pltpu.VMEM((2 * NX, plan.shape[1]) + cache.shape[1:], bf16),
            pltpu.VMEM((ny * nz,) + routes.shape, bf16),
            pltpu.VMEM((ny * nz * block, ny * nz * block), bf16),
            pltpu.VMEM((steps, NQ * cap, ny * nz * block), bf16),
            pltpu.VMEM((steps, ny * nz * block, NQ * cap), bf16),
            pltpu.VMEM((steps, ny * nz * block, NQ * cap), bf16),
            pltpu.VMEM((2, NX * cap, hidden), bf16),
            pltpu.VMEM((steps, ny * nz, block, quarter), bf16),
            pltpu.VMEM((steps, 2 * NX, NQ * cap, quarter), bf16),
            pltpu.VMEM((steps, 2 * NX, NQ * cap, quarter), bf16),
            pltpu.VMEM((steps, NX, NQ * cap, quarter), bf16),
            pltpu.VMEM((steps, 2, NQ * cap // 2, quarter), bf16),
            pltpu.VMEM((steps, 2, NQ * cap, quarter), bf16),
            pltpu.VMEM((NQ * cap, quarter), bf16),
            pltpu.VMEM((steps, ny * nz, block, quarter), bf16),
            pltpu.VMEM((steps, max(ny - 1, 1), nz, block, quarter), bf16),
            pltpu.VMEM((steps, nz, block, quarter), bf16),
            pltpu.VMEM((steps, max(nz - 1, 1), block, quarter), bf16),
            pltpu.SemaphoreType.DMA((6,)),
            pltpu.SemaphoreType.DMA((copies,)),
            pltpu.SemaphoreType.DMA((copies,)),
        ],
        compiler_params=pltpu.CompilerParams(
            collective_id=0, has_side_effects=True, vmem_limit_bytes=60 << 20
        ),
    )(plan, lengths, tokens, routes, entries, queries, cache, w_gate, w_up, w_down)


def narrow(value):
    return lax.reduce_precision(value, exponent_bits=8, mantissa_bits=7)


def body(
    ny, queries, cache, new_entries, lengths, moe_input, expert_ids, route_gains,
    w_gate, w_up, w_down, plan,
):
    group = lax.axis_index("grp")
    nz = lax.axis_size("ep") // ny
    steps, owned, _ = moe_input.shape
    own_ids = lax.dynamic_index_in_dim(expert_ids, group, 1, keepdims=False)
    gains = lax.dynamic_index_in_dim(route_gains, group, 1, keepdims=False)
    top = own_ids.shape[2]
    first = narrow(gains)
    second = narrow(gains - first)
    third = gains - first - second
    routes = jnp.concatenate([own_ids.astype(jnp.float32), first, second, third], axis=2)
    routes = jnp.swapaxes(routes.astype(jnp.bfloat16), 0, 1).reshape(owned, -1)
    routes = jnp.pad(routes, ((0, 0), (0, 128 - routes.shape[1])))
    routes = jnp.broadcast_to(routes[None], (NQ, owned, 128)).reshape(-1, 128)
    out, migrated, contexts = layer_call(
        jnp.transpose(plan, (1, 2, 3, 0)), lengths, moe_input, routes, top, new_entries,
        jnp.swapaxes(queries, 2, 3), jnp.swapaxes(cache, 1, 2), w_gate, w_up, w_down, ny, nz,
    )
    return (contexts, jnp.swapaxes(migrated, 1, 2), out)


def solution(mesh):
    return jax.shard_map(
        partial(body, NY),
        mesh=mesh,
        in_specs=(
            P(None, ("grp", "ep"), None, None),
            P(("grp", "ep"), None, None),
            P(None, ("grp", "ep"), None),
            P(("grp", "ep")),
            P(None, ("grp", "ep"), None),
            P(None, None, "ep", None),
            P(None, None, "ep", None),
            P("ep", None, "grp"),
            P("ep", None, "grp"),
            P("ep", "grp", None),
            P(None, "ep", None, None),
        ),
        out_specs=(
            P(None, ("grp", "ep"), None, None),
            P(("grp", "ep"), None, None),
            P(None, ("grp", "ep"), None),
        ),
        check_vma=False,
    )
```
